512 devices in a mesh: dom: 128 (over x, z, core), sub: 4 (over y).
Axes of the slice: x: 4, y: 4, z: 16, core: 2. Of those that a mesh axis runs over, the one named last changes fastest.
Arguments:
- fine_residual: float32 [35, 5, 131072], P(None, None, ('dom', 'sub')), may hold values from -6 to 6
- fine_basis: float32 [64, 35], replicated, may hold values from -1 to 1
- coarse_basis: float32 [64, 10, 131072], P(None, None, ('dom', 'sub')), may hold values from -0.75 to 0.75
- donor_cells: int32 [131072, 4], P(('dom', 'sub')), may hold values from 0 to 65535, as said below
- point_counts: int32 [131072, 4], P(('dom', 'sub')), may hold values from 1 to 32, 64 in all within a row
- solver_pos: int32 [65536], P(('dom', 'sub')), may hold values from 0 to 65535, as said below
- block_inverse: float32 [50, 50, 65536], P(None, None, ('dom', 'sub')), may hold values from -0.25 to 1.65
- face_jacobian: float32 [4, 5, 5, 65536], P(None, None, None, ('dom', 'sub')), may hold values from -0.5 to 0.5
- face_lift: float32 [4, 10, 10], replicated, may hold values from -2 to 2
- face_offset: int32 [4, 65536], P(None, ('dom', 'sub')), may hold values from -32 to 32, as said below
Outputs:
- coarse_residual: float32 [50, 65536], P(None, ('dom', 'sub'))
- correction: float32 [50, 65536], P(None, ('dom', 'sub'))
The draws below stay inside these ranges and needn't reach their ends.
Inputs may be any that keep to these rules, and one draw needn't show every extreme that they name: `donor_cells`: among the 4 donors of the 256 fine elements of one device, at most 4 lie in any one block of 128 consecutive coarse elements; in 4 groups of 4 consecutive blocks every block receives exactly 4 from every device. `solver_pos`: A permutation; all 128 elements of one block go to one block of 128 solver positions in the same group of 4 consecutive blocks, distinct blocks to distinct ones. `face_offset`: 0 marks a boundary face, and so does a neighbour position outside 0 to 65535.
All inputs are finite; a program needn't handle non-finite values.
Results may differ from the reference program's by a relative error of at most 0.0003.
Values sent between devices are 32-bit elements; how exact they have to be, the bound alone decides.
A program may use at most 64 MiB of HBM per device.

```python
import math
import jax
import jax.numpy as jnp
import numpy as np
from jax import lax

MF = 35
MC = 10
NVAR = 5
NB = 50
Q = 64
K = 4
F_DEV = 256
C_DEV = 128
OWNERS = 512
NF = 131072
NC = 65536
CAP = 4
BUSYG = 4
REACH = 32
N_DOM = 128
N_SUB = 4


def draw_donor_cells(key, part):
    slot_total = OWNERS * CAP
    slot_owner = jnp.arange(slot_total, dtype=jnp.int32) // CAP
    group_pick = jax.random.permutation(jax.random.fold_in(key, 1), N_DOM)[:BUSYG]
    busy_group = jnp.zeros((N_DOM,), jnp.int32).at[group_pick].set(1)
    busy_slot = busy_group[slot_owner // N_SUB]

    def one_block(block_index):
        block_key = jax.random.fold_in(jax.random.fold_in(key, 2), block_index)
        random_score = jax.random.randint(jax.random.fold_in(block_key, 0), (slot_total,), 0, 2 ** 20)
        slot_score = random_score + (1 - busy_slot) * 2 ** 20
        chosen = jnp.argsort(slot_score, stable=True)[:F_DEV * K]
        shuffled = jax.random.permutation(jax.random.fold_in(block_key, 1), chosen)
        owner_block = slot_owner[shuffled]
        local_seat = jax.random.randint(jax.random.fold_in(block_key, 2), (F_DEV * K,), 0, C_DEV)
        return (owner_block * C_DEV + local_seat).reshape(F_DEV, K)
    return jax.vmap(one_block)(jnp.arange(OWNERS)).reshape(NF, K).astype(jnp.int32)


def draw_solver_pos(key, part):
    base_key = jax.random.fold_in(key, 11)

    def one_group(group_index):
        group_key = jax.random.fold_in(base_key, group_index)
        sub_order = jax.random.permutation(jax.random.fold_in(group_key, 0), N_SUB)
        inner_order = jax.vmap(lambda sub_index: jax.random.permutation(jax.random.fold_in(group_key, sub_index + 1), C_DEV))(jnp.arange(N_SUB))
        return ((group_index * N_SUB + sub_order)[:, None] * C_DEV + inner_order).reshape(N_SUB * C_DEV)
    return jax.vmap(one_group)(jnp.arange(N_DOM)).reshape(NC).astype(jnp.int32)


def draw_face_offset(key, part):
    base_key = jax.random.fold_in(key, 21)
    reach_size = jax.random.randint(jax.random.fold_in(base_key, 0), (4, NC), 1, REACH + 1)
    sign_choice = jax.random.randint(jax.random.fold_in(base_key, 1), (4, NC), 0, 2) * 2 - 1
    is_wall = jax.random.randint(jax.random.fold_in(base_key, 2), (4, NC), 0, 10) == 0
    return jnp.where(is_wall, 0, reach_size * sign_choice).astype(jnp.int32)


def draw_block_inverse(key, part):
    base_key = jax.random.fold_in(key, 31)
    identity = (jnp.arange(NB)[:, None] == jnp.arange(NB)[None, :]).astype(jnp.float32)[:, :, None]
    diagonal = jax.random.uniform(jax.random.fold_in(base_key, 0), (NB, 1, NC), jnp.float32, 0.6, 1.4)
    off_diagonal = jnp.clip(0.05 * jax.random.normal(jax.random.fold_in(base_key, 1), (NB, NB, NC), jnp.float32), -0.25, 0.25)
    return (identity * diagonal + off_diagonal).astype(jnp.float32)


def levels(stream_key, extent, shards, low, high):
    factor_of = 1.0
    for dim, blocks in shards:
        heights = jax.random.uniform(jax.random.fold_in(jax.random.fold_in(stream_key, 6), dim), (blocks,), jnp.float32, low / len(shards), high / len(shards))
        factor_of = factor_of * jnp.repeat(jnp.exp(heights), extent[dim] // blocks).reshape((-1,) + (1,) * (len(extent) - 1 - dim))
    return factor_of


def profile(number_of, total, limit, lean):
    weights = [(1 << 20) // math.isqrt(rank ** lean) + 1 for rank in range(2, number_of + 1)]
    spare, given = total - limit - (number_of - 1), [1] * (number_of - 1)
    while spare > 0:
        candidates = [i for i in range(number_of - 1) if given[i] < limit]
        mass, budget = sum([weights[i] for i in candidates]), spare
        for i in candidates:
            more = min(limit - given[i], max(1, budget * weights[i] // mass), spare)
            given[i] = given[i] + more
            spare = spare - more
    return np.array([limit] + given)


def ragged(rng, amount, total, reach, lean):
    if amount == 2:
        one = jax.random.randint(rng, (), max(1, total - reach), min(reach, total - 1) + 1)
        return jnp.stack([one, total - one])
    tallies = jnp.asarray(profile(amount, total, reach, lean), jnp.int32)
    twos = (amount - 1) // 2
    giver, taker = tallies[1:1 + 2 * twos:2], tallies[2:2 + 2 * twos:2]
    slack = jnp.minimum(giver - 1, reach - taker)
    shifted = jax.random.randint(jax.random.fold_in(rng, 1), (twos,), 0, 1 << 20) % (slack + 1)
    tallies = tallies.at[1:1 + 2 * twos:2].set(giver - shifted).at[2:2 + 2 * twos:2].set(taker + shifted)
    return tallies[jax.random.permutation(jax.random.fold_in(rng, 2), amount)]


def gaussian(own_key, extent, deviation, most, shards=(), kind=jnp.bfloat16):
    entries = jax.random.normal(own_key, extent, jnp.float32) * deviation
    if len(shards) > 0:
        entries = levels(own_key, extent, shards, -0.22, 0.18) * entries
    return jnp.clip(entries, min=-most, max=most).astype(kind)


def setup_inputs(seed: int = 0) -> dict:
    splits = jax.random.split(jax.random.key(seed), 11)
    return {
        "fine_residual": gaussian(splits[0], (MF, NVAR, NF), 1.0, 6.0, ((2, 512),), jnp.float32),
        "fine_basis": gaussian(splits[1], (Q, MF), MF ** -0.5, 1.0, (), jnp.float32),
        "coarse_basis": gaussian(splits[2], (Q, MC, NF), Q ** -0.5, 0.75, ((2, 512),), jnp.float32),
        "donor_cells": draw_donor_cells(jax.random.fold_in(splits[10], 71), 0),
        "point_counts": jax.vmap(lambda own: ragged(own, K, Q, Q // 2, 1))(jax.random.split(splits[4], NF)).reshape((NF, K)).astype(jnp.int32),
        "solver_pos": draw_solver_pos(jax.random.fold_in(splits[10], 71), 0),
        "block_inverse": draw_block_inverse(jax.random.fold_in(splits[10], 71), 0),
        "face_jacobian": gaussian(splits[7], (4, NVAR, NVAR, NC), 0.08, 0.5, ((3, 512),), jnp.float32),
        "face_lift": gaussian(splits[8], (4, MC, MC), MC ** -0.5, 2.0, (), jnp.float32),
        "face_offset": draw_face_offset(jax.random.fold_in(splits[10], 71), 0),
    }


def pair_terms(residual, fine_basis, coarse_basis, counts):
    mode_count, variables, fine_count = residual.shape
    point_total = fine_basis.shape[0]
    values = jnp.dot(fine_basis, residual.reshape(mode_count, variables * fine_count), precision=lax.Precision.HIGHEST, preferred_element_type=jnp.float32)
    values = values.reshape(point_total, variables, fine_count)
    upper_point = jnp.cumsum(counts, axis=1)
    lower_point = upper_point - counts
    points = jnp.arange(point_total, dtype=jnp.int32)[:, None]
    slot_terms = []
    for slot_index in range(counts.shape[1]):
        inside = (points >= lower_point[:, slot_index][None, :]) & (points < upper_point[:, slot_index][None, :])
        masked = jnp.where(inside[:, None, :], coarse_basis, jnp.float32(0.0))
        slot_terms.append(jnp.einsum("qae,qve->eav", masked, values, precision=lax.Precision.HIGHEST))
    stacked = jnp.stack(slot_terms, axis=1)
    return stacked.reshape(fine_count * counts.shape[1], -1)


def couple(coarse_field, face_jacobian, face_lift, face_offset):
    element_total = coarse_field.shape[1]
    own_index = jnp.arange(element_total, dtype=jnp.int32)
    result = jnp.zeros((MC, NVAR, element_total), jnp.float32)
    for face_index in range(4):
        offset_row = face_offset[face_index]
        neighbour = own_index + offset_row
        inside = (offset_row != 0) & (neighbour >= 0) & (neighbour < element_total)
        picked = jnp.where(inside[None, :], coarse_field[:, jnp.clip(neighbour, 0, element_total - 1)], jnp.float32(0.0))
        picked = picked.reshape(MC, NVAR, element_total)
        lifted = jnp.einsum("ab,bvp->avp", face_lift[face_index], picked, precision=lax.Precision.HIGHEST)
        result = result + jnp.einsum("avp,wvp->awp", lifted, face_jacobian[face_index], precision=lax.Precision.HIGHEST)
    return result.reshape(MC * NVAR, element_total)


def apply_inverse(block_inverse, coarse_field):
    return jnp.einsum("ijp,jp->ip", block_inverse, coarse_field, precision=lax.Precision.HIGHEST)


def reference(fine_residual, fine_basis, coarse_basis, donor_cells, point_counts, solver_pos, block_inverse, face_jacobian, face_lift, face_offset):
    blocks = fine_residual.shape[2] // F_DEV
    element_total = solver_pos.shape[0]
    residual_blocks = jnp.moveaxis(fine_residual.reshape(MF, NVAR, blocks, F_DEV), 2, 0)
    basis_blocks = jnp.moveaxis(coarse_basis.reshape(Q, MC, blocks, F_DEV), 2, 0)
    donor_blocks = donor_cells.reshape(blocks, F_DEV * K)
    count_blocks = point_counts.reshape(blocks, F_DEV, K)

    def accumulate(restricted, block_items):
        residual, basis, donors, counts = block_items
        pair_values = pair_terms(residual, fine_basis, basis, counts)
        return restricted.at[donors].add(pair_values), None

    restricted, unused = lax.scan(accumulate, jnp.zeros((element_total, MC * NVAR), jnp.float32), (residual_blocks, basis_blocks, donor_blocks, count_blocks))
    coarse_residual = jnp.zeros((element_total, MC * NVAR), jnp.float32).at[solver_pos].set(restricted).T
    first_sweep = apply_inverse(block_inverse, coarse_residual)
    second = apply_inverse(block_inverse, coarse_residual - couple(first_sweep, face_jacobian, face_lift, face_offset))
    third_sweep = apply_inverse(block_inverse, coarse_residual - couple(second, face_jacobian, face_lift, face_offset))
    return coarse_residual, third_sweep
```

```python
import functools

import jax
import jax.numpy as jnp
from jax import lax
from jax.experimental import pallas as pl
from jax.experimental.pallas import tpu as pltpu
from jax.sharding import PartitionSpec as P

MESH = pl.DeviceIdType.MESH
F32 = jnp.float32
BF16 = jnp.bfloat16

NZ = 16
NP = 32
NY = 4
ROWS = 56
PIECES = ((0, 32), (32, 24))


def halves(value):
    high = value.astype(BF16)
    return high, (value - high.astype(F32)).astype(BF16)


def dot_nt(left, right):
    return lax.dot_general(left, right, (((1,), (1,)), ((), ())), preferred_element_type=F32)


def dot_nn(left, right):
    return lax.dot_general(left, right, (((1,), (0,)), ((), ())), preferred_element_type=F32)


def ones_where(mask):
    return jnp.where(mask, F32(1.0), F32(0.0))


def iota(shape, dim):
    return lax.broadcasted_iota(jnp.int32, shape, dim)


def kernel(
    residual_hbm,
    fine_basis,
    basis_hbm,
    donors,
    counts,
    positions,
    inverse_hbm,
    jacobian,
    lift,
    offsets,
    coarse_out,
    correction_out,
    residual,
    basis,
    inverse,
    masked,
    pair,
    spread,
    outbox,
    inbox,
    chunks,
    ring_up,
    ring_down,
    group,
    group_pos,
    seats_to_pos,
    chooser,
    lift_rows,
    iterate,
    halo_low,
    halo_high,
    coupling,
    load_sem,
    plane_send,
    plane_recv,
    up_send,
    up_recv,
    down_send,
    down_recv,
    group_send,
    group_recv,
    pos_send,
    pos_recv,
    halo_send,
    halo_recv,
):
    dom = lax.axis_index("dom")
    y = lax.axis_index("sub")
    x = lax.div(dom, 32)
    z = lax.rem(lax.div(dom, 2), NZ)
    core = lax.rem(dom, 2)
    me = x * 8 + core * 4 + y
    block = dom * NY + y

    def plane_peer(step):
        other = lax.rem(me + step, NP)
        far_x = lax.div(other, 8)
        far_core = lax.rem(lax.div(other, 4), 2)
        return ((far_x * NZ + z) * 2 + far_core, lax.rem(other, NY))

    def ring_peer(step):
        return ((x * NZ + lax.rem(z + step, NZ)) * 2 + core, y)

    def group_peer(step):
        return (dom, lax.rem(y + step, NY))

    def line_peer(step):
        other = lax.rem(block + step, 512)
        return (lax.div(other, NY), lax.rem(other, NY))

    load_residual = pltpu.make_async_copy(residual_hbm, residual, load_sem.at[0])
    load_basis = pltpu.make_async_copy(basis_hbm, basis, load_sem.at[1])
    load_inverse = pltpu.make_async_copy(inverse_hbm, inverse, load_sem.at[2])
    load_residual.start()
    load_basis.start()
    load_inverse.start()

    barrier = pltpu.get_barrier_semaphore()

    def greet(step, carry):
        pl.semaphore_signal(barrier, inc=1, device_id=plane_peer(step), device_id_type=MESH)
        return carry

    lax.fori_loop(1, NP, greet, 0)
    for peer in (ring_peer(1), ring_peer(NZ - 1), line_peer(1), line_peer(511)):
        pl.semaphore_signal(barrier, inc=1, device_id=peer, device_id_type=MESH)

    donor_row = jnp.concatenate([donors[k : k + 1, :] for k in range(4)], axis=1)
    owner = lax.shift_right_logical(donor_row, 7)
    seat = jnp.bitwise_and(donor_row, 127).astype(F32)
    owner_f = owner.astype(F32)
    columns = []
    for tile in range(8):
        row = owner_f[:, tile * 128 : (tile + 1) * 128]
        columns.append(jnp.broadcast_to(row, (128, 128)).T)
    earlier = iota((128, 128), 0) < iota((128, 128), 1)
    ranks = []
    for tile in range(8):
        row = owner_f[:, tile * 128 : (tile + 1) * 128]
        total = ones_where((columns[tile] == row) & earlier)
        for before in range(tile):
            total = total + ones_where(columns[before] == row)
        ranks.append(jnp.sum(total, axis=0, keepdims=True))
    rank = jnp.concatenate(ranks, axis=1).astype(jnp.int32)
    far_plane = lax.shift_right_logical(owner, 7) * 8 + jnp.bitwise_and(owner, 7)
    far_z = jnp.bitwise_and(lax.shift_right_logical(owner, 3), 15)
    plane_step = jnp.bitwise_and(far_plane - me + NP, NP - 1)
    order = jnp.bitwise_and(far_z - z + 11 + NZ, NZ - 1)
    slot = plane_step * 32 + lax.shift_right_logical(order, 1) * 4 + rank
    odd = jnp.bitwise_and(order, 1)
    slot_even = jnp.where(odd == 0, slot, -1)
    slot_odd = jnp.where(odd == 1, slot, -1)

    upper0 = counts[0:1, :]
    upper1 = upper0 + counts[1:2, :]
    upper2 = upper1 + counts[2:3, :]
    point = iota((64, 256), 0)
    inside = (
        point < upper0,
        (point >= upper0) & (point < upper1),
        (point >= upper1) & (point < upper2),
        point >= upper2,
    )
    spans = ((0, 32), (0, 64), (0, 64), (32, 64))
    load_residual.wait()
    fine = fine_basis[...].T
    for v in range(5):
        values = lax.dot_general(
            fine,
            residual[v],
            (((1,), (0,)), ((), ())),
            precision=lax.Precision.HIGHEST,
            preferred_element_type=F32,
        )
        for k in range(4):
            masked[k, v] = jnp.where(inside[k], values, F32(0.0))
    load_basis.wait()
    for a in range(10):
        for k in range(4):
            low, high = spans[k]
            product = basis[a, low:high, :][None] * masked[k, :, low:high, :]
            pair[a * 5 : a * 5 + 5, k * 256 : (k + 1) * 256] = jnp.sum(product, axis=1)
    pair[50:51, :] = seat
    pair[51:64, :] = jnp.zeros((13, 1024), F32)
    pair_high, pair_low = halves(pair[...])
    nothing = jnp.zeros((64, 1024), BF16)
    spread[0] = jnp.concatenate([pair_high, nothing, pair_low, nothing], axis=0)
    spread[1] = jnp.concatenate([nothing, pair_high, nothing, pair_low], axis=0)

    pl.semaphore_wait(barrier, 35)

    group_pos[0] = jnp.broadcast_to(positions[...], (8, 128))

    def pos_copy(step):
        return pltpu.make_async_remote_copy(
            src_ref=group_pos.at[0],
            dst_ref=group_pos.at[step],
            send_sem=pos_send.at[step],
            recv_sem=pos_recv.at[step],
            device_id=group_peer(step),
            device_id_type=MESH,
        )

    for step in range(1, NY):
        pos_copy(step).start()

    def plane_copy(half, step):
        return pltpu.make_async_remote_copy(
            src_ref=outbox.at[step, pl.ds(half * 2, 2)],
            dst_ref=inbox.at[pl.ds(half * 2, 2), step],
            send_sem=plane_send.at[half, step],
            recv_sem=plane_recv.at[half, step],
            device_id=plane_peer(step),
            device_id_type=MESH,
        )

    def start_plane(half):
        def body(step, carry):
            plane_copy(half, step).start()
            return carry

        return body

    for part in range(4):
        slots = iota((256, 1024), 0) + part * 256
        rows = dot_nt(ones_where(slots == slot_even).astype(BF16), spread[0])
        rows = rows + dot_nt(ones_where(slots == slot_odd).astype(BF16), spread[1])
        rows = rows[:, :128] + rows[:, 128:]
        outbox[part * 8 : (part + 1) * 8] = rows.reshape(8, 4, 8, 128)
        lax.fori_loop(max(1, part * 8), part * 8 + 8, start_plane(0), 0)
    lax.fori_loop(1, NP, start_plane(1), 0)
    inbox[:, 0] = outbox[0]

    for half in range(3):
        source = iota((128, 128), 0) + half * 128
        for f in range(4):
            offset = offsets[f : f + 1, :]
            own = iota((1, 128), 1)
            there = block * 128 + own + offset
            good = (offset != 0) & (there >= 0) & (there < 65536)
            wanted = jnp.where(good, own + offset + 128, -1)
            chooser[half * 128 : half * 128 + 128, f * 128 : f * 128 + 128] = ones_where(
                source == wanted
            ).astype(BF16)
    row_v = lax.shift_right_logical(iota((80, 64), 0), 4)
    col = iota((80, 64), 1)
    fifth = jnp.zeros((80, 64), jnp.int32)
    for b in range(1, 10):
        fifth = fifth + jnp.where(col >= b * 5, 1, 0)
    same = (col - fifth * 5 == row_v) & (col < 50)
    take_a = ones_where(
        jnp.bitwise_and(iota((80, 10), 0), 15) == iota((80, 10), 1)
    ).astype(BF16)
    b_low = iota((10, 64), 0) * 5
    b_col = iota((10, 64), 1)
    take_b = ones_where((b_col >= b_low) & (b_col < b_low + 5)).astype(BF16)
    for f in range(4):
        for n, part in enumerate(halves(lift[:, f, :])):
            wide = dot_nn(dot_nn(take_a, part).astype(BF16), take_b)
            wide = jnp.where(same, wide, F32(0.0)).astype(BF16)
            lift_rows[f, n * 80 : n * 80 + 80, :] = jnp.concatenate([wide, wide], axis=1)
    for it in range(2):
        iterate[it, 48:64, :] = jnp.zeros((16, 128), F32)
    for step in range(1, NY):
        pos_copy(step).wait_recv()
    place = iota((128, 128), 0) + block * 128
    for step in range(NY):
        seats_to_pos[:, step * 128 : step * 128 + 128] = ones_where(
            place == group_pos[step, 0:1, :]
        ).astype(BF16)

    def wait_plane(half):
        def body(step, carry):
            plane_copy(half, step).wait_recv()
            return carry

        lax.fori_loop(1, NP, body, 0)

    in_pair = jnp.bitwise_and(lax.shift_right_logical(iota((128, 256), 1), 2), 1)
    cell = iota((128, 256), 0).astype(F32)

    def gather(quarter):
        turned = inbox[quarter].reshape(256, 128).T
        high, low = halves(turned)
        for h in range(2):
            left = jnp.concatenate(
                [high[h * 64 : h * 64 + 64], low[h * 64 : h * 64 + 64]], axis=0
            )
            hit = cell == turned[h * 64 + 50 : h * 64 + 51, :]
            right = jnp.concatenate(
                [
                    ones_where(hit & (in_pair == 0)).astype(BF16),
                    ones_where(hit & (in_pair == 1)).astype(BF16),
                ],
                axis=0,
            )
            both = dot_nt(left, right)
            both = both[:64] + both[64:]
            for n in range(2):
                chunks[quarter * 4 + n * 2 + h] = both[:, n * 128 : n * 128 + 128]

    def chunk_of(relative):
        return (relative + 11) % 16

    def ring_copy(s, piece, up):
        start, size = PIECES[piece]
        relative = 8 - s if up else s - 7
        return pltpu.make_async_remote_copy(
            src_ref=chunks.at[chunk_of(relative), pl.ds(start, size)],
            dst_ref=(ring_up if up else ring_down).at[s, pl.ds(start, size)],
            send_sem=(up_send if up else down_send).at[s, piece],
            recv_sem=(up_recv if up else down_recv).at[s, piece],
            device_id=ring_peer(1 if up else NZ - 1),
            device_id_type=MESH,
        )

    wait_plane(0)
    gather(0)
    gather(1)
    for s in range(8):
        for piece, (start, size) in enumerate(PIECES):
            for up in (True, False):
                if not up and s == 7:
                    continue
                if s:
                    ring_copy(s - 1, piece, up).wait_recv()
                    index = chunk_of(8 - s if up else s - 7)
                    arrived = (ring_up if up else ring_down)[s - 1, start : start + size, :]
                    chunks[index, start : start + size, :] += arrived
                ring_copy(s, piece, up).start()
        if s == 2:
            wait_plane(1)
            gather(2)
        if s == 3:
            gather(3)

    def group_copy(step, piece):
        start, size = PIECES[piece]
        return pltpu.make_async_remote_copy(
            src_ref=group.at[0, pl.ds(start, size)],
            dst_ref=group.at[step, pl.ds(start, size)],
            send_sem=group_send.at[step, piece],
            recv_sem=group_recv.at[step, piece],
            device_id=group_peer(step),
            device_id_type=MESH,
        )

    for piece, (start, size) in enumerate(PIECES):
        ring_copy(6, piece, False).wait_recv()
        mine = chunks[chunk_of(0), start : start + size, :] + ring_down[6, start : start + size, :]
        ring_copy(7, piece, True).wait_recv()
        group[0, start : start + size, :] = mine + ring_up[7, start : start + size, :]
        for step in range(1, NY):
            group_copy(step, piece).start()
    load_inverse.wait()
    for piece in range(len(PIECES)):
        for step in range(1, NY):
            group_copy(step, piece).wait_recv()
    blank = jnp.zeros((8, 128), F32)
    wide = jnp.concatenate(
        [jnp.concatenate([group[step], blank], axis=0) for step in range(NY)], axis=1
    )
    high, low = halves(wide)
    coarse = dot_nt(jnp.concatenate([high, low], axis=0), seats_to_pos[...])
    coarse = (coarse[:64] + coarse[64:])[:50]
    coarse_out[...] = coarse

    def apply_inverse(field):
        return jnp.sum(inverse[...] * field[None], axis=1)

    def halo_copy(it, up):
        return pltpu.make_async_remote_copy(
            src_ref=iterate.at[it, pl.ds(0, ROWS)],
            dst_ref=(halo_low if up else halo_high).at[it],
            send_sem=halo_send.at[it, 0 if up else 1],
            recv_sem=halo_recv.at[it, 0 if up else 1],
            device_id=line_peer(1 if up else 511),
            device_id_type=MESH,
        )

    field = apply_inverse(coarse)
    for it in range(2):
        iterate[it, 0:50, :] = field
        halo_copy(it, True).start()
        halo_copy(it, False).start()
        halo_copy(it, True).wait_recv()
        halo_copy(it, False).wait_recv()
        wide = jnp.concatenate(
            [
                jnp.concatenate([halo_low[it], blank], axis=0),
                iterate[it],
                jnp.concatenate([halo_high[it], blank], axis=0),
            ],
            axis=1,
        )
        high, low = halves(wide)
        picked = dot_nn(jnp.concatenate([high, low], axis=0), chooser[...]).astype(BF16)
        lifted = []
        for f in range(4):
            both = dot_nn(lift_rows[f], picked[:, f * 128 : f * 128 + 128])
            lifted.append(both[:80] + both[80:])
        for w in range(5):
            total = jnp.zeros((16, 128), F32)
            for f in range(4):
                for v in range(5):
                    total = total + lifted[f][v * 16 : v * 16 + 16] * jacobian[w, v, f : f + 1, :]
            coupling[pl.ds(w, 10, stride=5), :] = total[:10]
        field = apply_inverse(coarse - coupling[0:50, :])
    correction_out[...] = field

    for half in range(2):

        def sent(step, carry, half=half):
            plane_copy(half, step).wait_send()
            return carry

        lax.fori_loop(1, NP, sent, 0)
    for s in range(8):
        for piece in range(len(PIECES)):
            ring_copy(s, piece, True).wait_send()
            if s < 7:
                ring_copy(s, piece, False).wait_send()
    for step in range(1, NY):
        pos_copy(step).wait_send()
        for piece in range(len(PIECES)):
            group_copy(step, piece).wait_send()
    for it in range(2):
        halo_copy(it, True).wait_send()
        halo_copy(it, False).wait_send()


def per_device(
    fine_residual,
    fine_basis,
    coarse_basis,
    donor_cells,
    point_counts,
    solver_pos,
    block_inverse,
    face_jacobian,
    face_lift,
    face_offset,
):
    vmem = pl.BlockSpec(memory_space=pltpu.VMEM)
    hbm = pl.BlockSpec(memory_space=pl.ANY)
    pieces = len(PIECES)
    dma = pltpu.SemaphoreType.DMA
    return pl.pallas_call(
        kernel,
        out_shape=(
            jax.ShapeDtypeStruct((50, 128), F32),
            jax.ShapeDtypeStruct((50, 128), F32),
        ),
        in_specs=[hbm, vmem, hbm, vmem, vmem, vmem, hbm, vmem, vmem, vmem],
        out_specs=(vmem, vmem),
        scratch_shapes=[
            pltpu.VMEM((5, 35, 256), F32),
            pltpu.VMEM((10, 64, 256), F32),
            pltpu.VMEM((50, 50, 128), F32),
            pltpu.VMEM((4, 5, 64, 256), F32),
            pltpu.VMEM((64, 1024), F32),
            pltpu.VMEM((2, 256, 1024), BF16),
            pltpu.VMEM((NP, 4, 8, 128), F32),
            pltpu.VMEM((4, NP, 8, 128), F32),
            pltpu.VMEM((NZ, 64, 128), F32),
            pltpu.VMEM((8, ROWS, 128), F32),
            pltpu.VMEM((7, ROWS, 128), F32),
            pltpu.VMEM((NY, ROWS, 128), F32),
            pltpu.VMEM((NY, 8, 128), jnp.int32),
            pltpu.VMEM((128, 512), BF16),
            pltpu.VMEM((384, 512), BF16),
            pltpu.VMEM((4, 160, 128), BF16),
            pltpu.VMEM((2, 64, 128), F32),
            pltpu.VMEM((2, ROWS, 128), F32),
            pltpu.VMEM((2, ROWS, 128), F32),
            pltpu.VMEM((64, 128), F32),
            dma((3,)),
            dma((2, NP)),
            dma((2, NP)),
            dma((8, pieces)),
            dma((8, pieces)),
            dma((7, pieces)),
            dma((7, pieces)),
            dma((NY, pieces)),
            dma((NY, pieces)),
            dma((NY,)),
            dma((NY,)),
            dma((2, 2)),
            dma((2, 2)),
        ],
        compiler_params=pltpu.CompilerParams(
            collective_id=0, has_side_effects=True, vmem_limit_bytes=40 * 1024 * 1024
        ),
    )(
        fine_residual.transpose(1, 0, 2),
        fine_basis.T,
        coarse_basis.transpose(1, 0, 2),
        donor_cells.T,
        point_counts.T,
        solver_pos.reshape(1, 128),
        block_inverse,
        face_jacobian.transpose(1, 2, 0, 3),
        face_lift.transpose(1, 0, 2),
        face_offset,
    )


def solution(mesh):
    in_specs = (
        P(None, None, ("dom", "sub")),
        P(),
        P(None, None, ("dom", "sub")),
        P(("dom", "sub"), None),
        P(("dom", "sub"), None),
        P(("dom", "sub")),
        P(None, None, ("dom", "sub")),
        P(None, None, None, ("dom", "sub")),
        P(),
        P(None, ("dom", "sub")),
    )
    out_specs = (P(None, ("dom", "sub")), P(None, ("dom", "sub")))
    return jax.shard_map(
        per_device, mesh=mesh, in_specs=in_specs, out_specs=out_specs, check_vma=False
    )
```

```python
import functools

import jax
import jax.numpy as jnp
from jax import lax
from jax.experimental import pallas as pl
from jax.experimental.pallas import tpu as pltpu
from jax.sharding import PartitionSpec as P

MESH = pl.DeviceIdType.MESH
F32 = jnp.float32
BF16 = jnp.bfloat16

NZ = 16
NP = 32
NY = 4
ROWS = 56
PARTS = (2, 1, 3, 0)
VIA = ((3, 8), (-3, -7), (2, 7), (-2, -6), (1, 6), (-1, -5))
LAST = (4, -3, 3, -2, 2, -1, 1, 5, -4)


def halves(value):
    high = value.astype(BF16)
    return high, (value - high.astype(F32)).astype(BF16)


def dot_nt(left, right):
    return lax.dot_general(left, right, (((1,), (1,)), ((), ())), preferred_element_type=F32)


def dot_nn(left, right):
    return lax.dot_general(left, right, (((1,), (0,)), ((), ())), preferred_element_type=F32)


def ones_where(mask):
    return jnp.where(mask, F32(1.0), F32(0.0))


def iota(shape, dim):
    return lax.broadcasted_iota(jnp.int32, shape, dim)


def kernel(
    residual_hbm,
    fine_basis_hbm,
    basis_hbm,
    donors_hbm,
    counts_hbm,
    positions_hbm,
    inverse_hbm,
    jacobian_hbm,
    lift_hbm,
    offsets_hbm,
    coarse_out,
    correction_out,
    residual,
    fine_basis,
    basis,
    donors,
    counts,
    positions,
    inverse,
    jacobian,
    lift,
    offsets,
    masked,
    pair,
    spread,
    outbox,
    inbox,
    chunks,
    via_in,
    last_in,
    group,
    group_pos,
    seats_to_pos,
    chooser,
    lift_rows,
    ends_high,
    ends_low,
    halo_low,
    halo_high,
    coupling,
    load_sem,
    plane_send,
    plane_recv,
    via_send,
    via_recv,
    last_send,
    last_recv,
    group_send,
    group_recv,
    pos_send,
    pos_recv,
    halo_send,
    halo_recv,
):
    dom = lax.axis_index("dom")
    y = lax.axis_index("sub")
    x = lax.div(dom, 32)
    z = lax.rem(lax.div(dom, 2), NZ)
    core = lax.rem(dom, 2)
    block = dom * NY + y

    def plane_peer(step):
        far_x = lax.rem(x + lax.div(step, 8), 4)
        far_core = lax.rem(core + lax.div(step, 4), 2)
        far_y = lax.rem(y + step, NY)
        return ((far_x * NZ + z) * 2 + far_core, far_y)

    def ring_peer(step):
        return ((x * NZ + lax.rem(z + step, NZ)) * 2 + core, y)

    def group_peer(step):
        return (dom, lax.rem(y + step, NY))

    def line_peer(step):
        other = lax.rem(block + step, 512)
        return (lax.div(other, NY), lax.rem(other, NY))

    loads = [
        pltpu.make_async_copy(source, target, load_sem.at[n])
        for n, (source, target) in enumerate(
            (
                (donors_hbm, donors),
                (counts_hbm, counts),
                (fine_basis_hbm, fine_basis),
                (residual_hbm, residual),
                (basis_hbm, basis),
                (positions_hbm, positions),
                (offsets_hbm, offsets),
                (lift_hbm, lift),
                (jacobian_hbm, jacobian),
                (inverse_hbm, inverse),
            )
        )
    ]
    for load in loads:
        load.start()

    barrier = pltpu.get_barrier_semaphore()

    for step in (5, 11, 4, 12, 3, 13, 2, 14, 1, 15):
        pl.semaphore_signal(barrier, inc=1, device_id=ring_peer(step), device_id_type=MESH)

    def plane_steps(part, body):
        def turned(i, carry):
            body(part * 8 + lax.rem(i, 2) * 4 + lax.rem(2 + 3 * lax.div(i, 2), NY))
            return carry

        def near(step, carry):
            body(step)
            return carry

        if part:
            lax.fori_loop(0, 8, turned, 0)
        else:
            lax.fori_loop(1, 8, near, 0)

    def greet(step):
        pl.semaphore_signal(barrier, inc=1, device_id=plane_peer(step), device_id_type=MESH)

    for part in PARTS:
        plane_steps(part, greet)
    for step in (1, 511):
        pl.semaphore_signal(barrier, inc=1, device_id=line_peer(step), device_id_type=MESH)

    loads[0].wait()
    donor_row = jnp.concatenate([donors[k : k + 1, :] for k in range(4)], axis=1)
    owner = lax.shift_right_logical(donor_row, 7)
    seat = jnp.bitwise_and(donor_row, 127).astype(F32)
    owner_f = owner.astype(F32)
    columns = []
    for tile in range(8):
        row = owner_f[:, tile * 128 : (tile + 1) * 128]
        columns.append(jnp.broadcast_to(row, (128, 128)).T)
    earlier = iota((128, 128), 0) < iota((128, 128), 1)
    ranks = []
    for tile in range(8):
        row = owner_f[:, tile * 128 : (tile + 1) * 128]
        total = ones_where((columns[tile] == row) & earlier)
        for before in range(tile):
            total = total + ones_where(columns[before] == row)
        ranks.append(jnp.sum(total, axis=0, keepdims=True))
    rank = jnp.concatenate(ranks, axis=1).astype(jnp.int32)
    far_z = jnp.bitwise_and(lax.shift_right_logical(owner, 3), 15)
    step_x = jnp.bitwise_and(lax.shift_right_logical(owner, 7) - x + 4, 3)
    step_core = jnp.bitwise_and(lax.shift_right_logical(owner, 2) - core + 2, 1)
    step_y = jnp.bitwise_and(owner - y + 4, 3)
    plane_step = step_x * 8 + step_core * 4 + step_y
    order = jnp.bitwise_and(far_z - z + 11 + NZ, NZ - 1)
    slot = plane_step * 32 + lax.shift_right_logical(order, 1) * 4 + rank
    odd = jnp.bitwise_and(order, 1)
    slot_even = jnp.where(odd == 0, slot, -1)
    slot_odd = jnp.where(odd == 1, slot, -1)

    for load in loads[1:4]:
        load.wait()
    upper0 = counts[0:1, :]
    upper1 = upper0 + counts[1:2, :]
    upper2 = upper1 + counts[2:3, :]
    point = iota((64, 256), 0)
    inside = (
        point < upper0,
        (point >= upper0) & (point < upper1),
        (point >= upper1) & (point < upper2),
        point >= upper2,
    )
    spans = ((0, 32), (0, 64), (0, 64), (32, 64))
    fine = fine_basis[...].T
    for v in range(5):
        values = lax.dot_general(
            fine,
            residual[v],
            (((1,), (0,)), ((), ())),
            precision=lax.Precision.HIGHEST,
            preferred_element_type=F32,
        )
        for k in range(4):
            masked[k, v] = jnp.where(inside[k], values, F32(0.0))
    loads[4].wait()
    for a in range(10):
        for k in range(4):
            low, high = spans[k]
            product = basis[a, low:high, :][None] * masked[k, :, low:high, :]
            pair[a * 5 : a * 5 + 5, k * 256 : (k + 1) * 256] = jnp.sum(product, axis=1)
    pair[50:51, :] = seat
    pair[51:64, :] = jnp.zeros((13, 1024), F32)
    pair_high, pair_low = halves(pair[...])
    nothing = jnp.zeros((64, 1024), BF16)
    spread[0] = jnp.concatenate([pair_high, nothing, pair_low, nothing], axis=0)
    spread[1] = jnp.concatenate([nothing, pair_high, nothing, pair_low], axis=0)

    for part in PARTS:
        slots = iota((256, 1024), 0) + part * 256
        rows = dot_nt(ones_where(slots == slot_even).astype(BF16), spread[0])
        rows = rows + dot_nt(ones_where(slots == slot_odd).astype(BF16), spread[1])
        rows = rows[:, :128] + rows[:, 128:]
        outbox[part * 8 : (part + 1) * 8] = rows.reshape(8, 4, 8, 128)

    pl.semaphore_wait(barrier, 43)
    loads[5].wait()

    group_pos[0] = jnp.broadcast_to(positions[...], (8, 128))

    def pos_copy(step):
        return pltpu.make_async_remote_copy(
            src_ref=group_pos.at[0],
            dst_ref=group_pos.at[step],
            send_sem=pos_send.at[step],
            recv_sem=pos_recv.at[step],
            device_id=group_peer(step),
            device_id_type=MESH,
        )

    def plane_copy(half, step):
        return pltpu.make_async_remote_copy(
            src_ref=outbox.at[step, pl.ds(half * 2, 2)],
            dst_ref=inbox.at[pl.ds(half * 2, 2), step],
            send_sem=plane_send.at[half],
            recv_sem=plane_recv.at[half],
            device_id=plane_peer(step),
            device_id_type=MESH,
        )

    for half in range(2):
        for part in PARTS:
            plane_steps(part, lambda step, half=half: plane_copy(half, step).start())
    for step in range(1, NY):
        pos_copy(step).start()
    inbox[:, 0] = outbox[0]

    for load in loads[6:8]:
        load.wait()
    own = iota((1, 128), 1)
    for f in range(4):
        offset = offsets[f : f + 1, :]
        there = block * 128 + own + offset
        good = (offset != 0) & (there >= 0) & (there < 65536)
        near = own + offset
        beyond = jnp.where(near < 0, near + 256, near)
        wanted = jnp.where(good, beyond, -1)
        for half in range(2):
            source = iota((128, 128), 0) + half * 128
            chooser[half * 128 : half * 128 + 128, f * 128 : f * 128 + 128] = ones_where(
                source == wanted
            ).astype(BF16)
    row_v = lax.shift_right_logical(iota((80, 64), 0), 4)
    col = iota((80, 64), 1)
    fifth = jnp.zeros((80, 64), jnp.int32)
    for b in range(1, 10):
        fifth = fifth + jnp.where(col >= b * 5, 1, 0)
    same = (col - fifth * 5 == row_v) & (col < 50)
    take_a = ones_where(
        jnp.bitwise_and(iota((80, 10), 0), 15) == iota((80, 10), 1)
    ).astype(BF16)
    b_low = iota((10, 64), 0) * 5
    b_col = iota((10, 64), 1)
    take_b = ones_where((b_col >= b_low) & (b_col < b_low + 5)).astype(BF16)
    for f in range(4):
        for n, part in enumerate(halves(lift[:, f, :])):
            wide = dot_nn(dot_nn(take_a, part).astype(BF16), take_b)
            wide = jnp.where(same, wide, F32(0.0)).astype(BF16)
            lift_rows[f, n * 80 : n * 80 + 80, :] = jnp.concatenate([wide, wide], axis=1)
    for step in range(1, NY):
        pos_copy(step).wait_recv()
    place = iota((128, 128), 0) + block * 128
    for step in range(NY):
        seats_to_pos[:, step * 128 : step * 128 + 128] = ones_where(
            place == group_pos[step, 0:1, :]
        ).astype(BF16)

    def wait_plane(half, sems):
        whole = inbox.at[pl.ds(half * 2, 2), pl.ds(1, NP - 1)]
        pltpu.make_async_copy(whole, whole, sems.at[half]).wait()

    in_pair = jnp.bitwise_and(lax.shift_right_logical(iota((128, 256), 1), 2), 1)
    cell = iota((128, 256), 0).astype(F32)

    def gather(quarter):
        turned = inbox[quarter].reshape(256, 128).T
        high, low = halves(turned)
        for h in range(2):
            left = jnp.concatenate(
                [high[h * 64 : h * 64 + 64], low[h * 64 : h * 64 + 64]], axis=0
            )
            hit = cell == turned[h * 64 + 50 : h * 64 + 51, :]
            right = jnp.concatenate(
                [
                    ones_where(hit & (in_pair == 0)).astype(BF16),
                    ones_where(hit & (in_pair == 1)).astype(BF16),
                ],
                axis=0,
            )
            both = dot_nt(left, right)
            both = both[:64] + both[64:]
            for n in range(2):
                chunks[quarter * 4 + n * 2 + h] = both[:, n * 128 : n * 128 + 128]

    def chunk_of(relative):
        return (relative + 11) % 16

    def via_copy(n):
        step, relative = VIA[n]
        return pltpu.make_async_remote_copy(
            src_ref=chunks.at[chunk_of(relative), pl.ds(0, ROWS)],
            dst_ref=via_in.at[n],
            send_sem=via_send.at[n],
            recv_sem=via_recv.at[n],
            device_id=ring_peer(step % NZ),
            device_id_type=MESH,
        )

    def last_copy(n):
        relative = LAST[n]
        return pltpu.make_async_remote_copy(
            src_ref=chunks.at[chunk_of(relative), pl.ds(0, ROWS)],
            dst_ref=last_in.at[n],
            send_sem=last_send.at[n],
            recv_sem=last_recv.at[n],
            device_id=ring_peer(relative % NZ),
            device_id_type=MESH,
        )

    wait_plane(0, plane_recv)
    gather(0)
    for n in (0, 2, 4):
        via_copy(n).start()
    gather(1)
    for n in (1, 3, 5):
        via_copy(n).start()
    wait_plane(1, plane_recv)
    gather(2)
    gather(3)
    for n in range(7):
        last_copy(n).start()
    for n in range(6):
        via_copy(n).wait_recv()
    for first, relative in ((0, 5), (1, -4)):
        added = via_in[first] + via_in[first + 2] + via_in[first + 4]
        chunks[chunk_of(relative), 0:ROWS, :] += added
    for n in (7, 8):
        last_copy(n).start()
    def group_copy(step):
        return pltpu.make_async_remote_copy(
            src_ref=group.at[0],
            dst_ref=group.at[step],
            send_sem=group_send.at[step],
            recv_sem=group_recv.at[step],
            device_id=group_peer(step),
            device_id_type=MESH,
        )

    mine = chunks[chunk_of(0), 0:ROWS, :]
    for n in range(9):
        last_copy(n).wait_recv()
        mine = mine + last_in[n]
    group[0] = mine
    for step in (2, 1, 3):
        group_copy(step).start()
    for load in loads[8:]:
        load.wait()
    for step in (1, 3, 2):
        group_copy(step).wait_recv()
    blank = jnp.zeros((8, 128), F32)
    wide = jnp.concatenate(
        [jnp.concatenate([group[step], blank], axis=0) for step in range(NY)], axis=1
    )
    high, low = halves(wide)
    coarse = dot_nt(jnp.concatenate([high, low], axis=0), seats_to_pos[...])
    coarse = (coarse[:64] + coarse[64:])[:50]
    coarse_out[...] = coarse

    def apply_inverse(field):
        return jnp.sum(inverse[...] * field[None], axis=1)

    def halo_copy(it, up):
        return pltpu.make_async_remote_copy(
            src_ref=(ends_high if up else ends_low).at[it],
            dst_ref=(halo_low if up else halo_high).at[it],
            send_sem=halo_send.at[it, 0 if up else 1],
            recv_sem=halo_recv.at[it, 0 if up else 1],
            device_id=line_peer(1 if up else 511),
            device_id_type=MESH,
        )

    lane_part = lax.shift_right_logical(iota((16, 128), 1), 5)

    def packed(rows, from_part):
        total = jnp.zeros((16, 128), F32)
        for g in range(4):
            shift = (g - from_part) % 4 * 32
            group_rows = rows[g * 16 : g * 16 + 16]
            turned = pltpu.roll(group_rows, shift, 1) if shift else group_rows
            total = jnp.where(lane_part == g, turned, total)
        return total

    def unpacked(low_ends, high_ends):
        parts = []
        for g in range(4):
            low_shift = (3 - g) % 4 * 32
            high_shift = (4 - g) % 4 * 32
            low_rows = pltpu.roll(low_ends, low_shift, 1) if low_shift else low_ends
            high_rows = pltpu.roll(high_ends, high_shift, 1) if high_shift else high_ends
            parts.append(jnp.where(lane_part == 3, low_rows, jnp.where(lane_part == 0, high_rows, F32(0.0))))
        return jnp.concatenate(parts, axis=0)

    field = apply_inverse(coarse)
    tail = jnp.zeros((14, 128), F32)
    for it in range(2):
        whole = jnp.concatenate([field, tail], axis=0)
        ends_high[it] = packed(whole, 3)
        ends_low[it] = packed(whole, 0)
        halo_copy(it, True).start()
        halo_copy(it, False).start()
        halo_copy(it, True).wait_recv()
        halo_copy(it, False).wait_recv()
        wide = jnp.concatenate([whole, unpacked(halo_low[it], halo_high[it])], axis=1)
        high, low = halves(wide)
        picked = dot_nn(jnp.concatenate([high, low], axis=0), chooser[...]).astype(BF16)
        lifted = []
        for f in range(4):
            both = dot_nn(lift_rows[f], picked[:, f * 128 : f * 128 + 128])
            lifted.append(both[:80] + both[80:])
        for w in range(5):
            total = jnp.zeros((16, 128), F32)
            for f in range(4):
                for v in range(5):
                    total = total + lifted[f][v * 16 : v * 16 + 16] * jacobian[w, v, f : f + 1, :]
            coupling[pl.ds(w, 10, stride=5), :] = total[:10]
        field = apply_inverse(coarse - coupling[0:50, :])
    correction_out[...] = field

    for half in range(2):
        wait_plane(half, plane_send)
    for n in range(6):
        via_copy(n).wait_send()
    for n in range(9):
        last_copy(n).wait_send()
    for step in range(1, NY):
        pos_copy(step).wait_send()
        group_copy(step).wait_send()
    for it in range(2):
        halo_copy(it, True).wait_send()
        halo_copy(it, False).wait_send()


def per_device(
    fine_residual,
    fine_basis,
    coarse_basis,
    donor_cells,
    point_counts,
    solver_pos,
    block_inverse,
    face_jacobian,
    face_lift,
    face_offset,
):
    vmem = pl.BlockSpec(memory_space=pltpu.VMEM)
    hbm = pl.BlockSpec(memory_space=pl.ANY)
    dma = pltpu.SemaphoreType.DMA
    return pl.pallas_call(
        kernel,
        out_shape=(
            jax.ShapeDtypeStruct((50, 128), F32),
            jax.ShapeDtypeStruct((50, 128), F32),
        ),
        in_specs=[hbm] * 10,
        out_specs=(vmem, vmem),
        scratch_shapes=[
            pltpu.VMEM((5, 35, 256), F32),
            pltpu.VMEM((35, 64), F32),
            pltpu.VMEM((10, 64, 256), F32),
            pltpu.VMEM((4, 256), jnp.int32),
            pltpu.VMEM((4, 256), jnp.int32),
            pltpu.VMEM((1, 128), jnp.int32),
            pltpu.VMEM((50, 50, 128), F32),
            pltpu.VMEM((5, 5, 4, 128), F32),
            pltpu.VMEM((10, 4, 10), F32),
            pltpu.VMEM((4, 128), jnp.int32),
            pltpu.VMEM((4, 5, 64, 256), F32),
            pltpu.VMEM((64, 1024), F32),
            pltpu.VMEM((2, 256, 1024), BF16),
            pltpu.VMEM((NP, 4, 8, 128), F32),
            pltpu.VMEM((4, NP, 8, 128), F32),
            pltpu.VMEM((NZ, 64, 128), F32),
            pltpu.VMEM((6, ROWS, 128), F32),
            pltpu.VMEM((9, ROWS, 128), F32),
            pltpu.VMEM((NY, ROWS, 128), F32),
            pltpu.VMEM((NY, 8, 128), jnp.int32),
            pltpu.VMEM((128, 512), BF16),
            pltpu.VMEM((256, 512), BF16),
            pltpu.VMEM((4, 160, 128), BF16),
            pltpu.VMEM((2, 16, 128), F32),
            pltpu.VMEM((2, 16, 128), F32),
            pltpu.VMEM((2, 16, 128), F32),
            pltpu.VMEM((2, 16, 128), F32),
            pltpu.VMEM((64, 128), F32),
            dma((10,)),
            dma((2,)),
            dma((2,)),
            dma((6,)),
            dma((6,)),
            dma((9,)),
            dma((9,)),
            dma((NY,)),
            dma((NY,)),
            dma((NY,)),
            dma((NY,)),
            dma((2, 2)),
            dma((2, 2)),
        ],
        compiler_params=pltpu.CompilerParams(
            collective_id=0, has_side_effects=True
        ),
    )(
        fine_residual.transpose(1, 0, 2),
        fine_basis.T,
        coarse_basis.transpose(1, 0, 2),
        donor_cells.T,
        point_counts.T,
        solver_pos.reshape(1, 128),
        block_inverse,
        face_jacobian.transpose(1, 2, 0, 3),
        face_lift.transpose(1, 0, 2),
        face_offset,
    )


def solution(mesh):
    in_specs = (
        P(None, None, ("dom", "sub")),
        P(),
        P(None, None, ("dom", "sub")),
        P(("dom", "sub"), None),
        P(("dom", "sub"), None),
        P(("dom", "sub")),
        P(None, None, ("dom", "sub")),
        P(None, None, None, ("dom", "sub")),
        P(),
        P(None, ("dom", "sub")),
    )
    out_specs = (P(None, ("dom", "sub")), P(None, ("dom", "sub")))
    return jax.shard_map(
        per_device, mesh=mesh, in_specs=in_specs, out_specs=out_specs, check_vma=False
    )
```

```python
import functools

import jax
import jax.numpy as jnp
from jax import lax
from jax.experimental import pallas as pl
from jax.experimental.pallas import tpu as pltpu
from jax.sharding import PartitionSpec as P

MESH = pl.DeviceIdType.MESH
F32 = jnp.float32
BF16 = jnp.bfloat16

NZ = 16
NP = 32
NY = 4
ROWS = 50
PARTS = (2, 1, 3, 0)
HOPS = (
    ((2, 8), (1, 7), (-1, -7)),
    ((2, 5), (1, 4), (-2, -5), (-1, -4), (3, 6), (-3, -6)),
    ((2, 2), (1, 1), (-2, -2), (-1, -1), (3, 3), (-3, -3)),
)


def halves(value):
    high = value.astype(BF16)
    return high, (value - high.astype(F32)).astype(BF16)


def dot_nt(left, right):
    return lax.dot_general(left, right, (((1,), (1,)), ((), ())), preferred_element_type=F32)


def dot_nn(left, right):
    return lax.dot_general(left, right, (((1,), (0,)), ((), ())), preferred_element_type=F32)


def ones_where(mask):
    return jnp.where(mask, F32(1.0), F32(0.0))


def iota(shape, dim):
    return lax.broadcasted_iota(jnp.int32, shape, dim)


def kernel(
    residual_hbm,
    fine_basis_hbm,
    basis_hbm,
    donors_hbm,
    counts_hbm,
    positions_hbm,
    inverse_hbm,
    jacobian_hbm,
    lift_hbm,
    offsets_hbm,
    coarse_out,
    correction_out,
    residual,
    fine_basis,
    basis,
    donors,
    counts,
    positions,
    inverse,
    jacobian,
    lift,
    offsets,
    masked,
    pair,
    spread,
    outbox,
    inbox,
    chunks,
    hop_in,
    group,
    group_pos,
    seats_to_pos,
    chooser,
    lift_rows,
    ends_high,
    ends_low,
    halo_low,
    halo_high,
    coupling,
    load_sem,
    plane_send,
    plane_recv,
    hop_send,
    hop_recv,
    group_send,
    group_recv,
    pos_send,
    pos_recv,
    halo_send,
    halo_recv,
):
    dom = lax.axis_index("dom")
    y = lax.axis_index("sub")
    x = lax.div(dom, 32)
    z = lax.rem(lax.div(dom, 2), NZ)
    core = lax.rem(dom, 2)
    block = dom * NY + y

    def plane_peer(step):
        far_x = lax.rem(x + lax.div(step, 8), 4)
        far_core = lax.rem(core + lax.div(step, 4), 2)
        far_y = lax.rem(y + step, NY)
        return ((far_x * NZ + z) * 2 + far_core, far_y)

    def ring_peer(step):
        return ((x * NZ + lax.rem(z + step, NZ)) * 2 + core, y)

    def group_peer(step):
        return (dom, lax.rem(y + step, NY))

    def line_peer(step):
        other = lax.rem(block + step, 512)
        return (lax.div(other, NY), lax.rem(other, NY))

    loads = [
        pltpu.make_async_copy(source, target, load_sem.at[n])
        for n, (source, target) in enumerate(
            (
                (donors_hbm, donors),
                (counts_hbm, counts),
                (fine_basis_hbm, fine_basis),
                (residual_hbm, residual),
                (basis_hbm, basis),
                (positions_hbm, positions),
                (offsets_hbm, offsets),
                (lift_hbm, lift),
                (jacobian_hbm, jacobian),
                (inverse_hbm, inverse),
            )
        )
    ]
    for load in loads:
        load.start()

    barrier = pltpu.get_barrier_semaphore()

    for step in (3, 13, 2, 14, 1, 15):
        pl.semaphore_signal(barrier, inc=1, device_id=ring_peer(step), device_id_type=MESH)

    def plane_steps(part, body):
        def turned(i, carry):
            body(part * 8 + lax.rem(i, 2) * 4 + lax.rem(2 + 3 * lax.div(i, 2), NY))
            return carry

        def near(step, carry):
            body(step)
            return carry

        if part:
            lax.fori_loop(0, 8, turned, 0)
        else:
            lax.fori_loop(1, 8, near, 0)

    def greet(step):
        pl.semaphore_signal(barrier, inc=1, device_id=plane_peer(step), device_id_type=MESH)

    for part in PARTS:
        plane_steps(part, greet)
    for step in (1, 511):
        pl.semaphore_signal(barrier, inc=1, device_id=line_peer(step), device_id_type=MESH)

    loads[0].wait()
    donor_row = jnp.concatenate([donors[k : k + 1, :] for k in range(4)], axis=1)
    owner = lax.shift_right_logical(donor_row, 7)
    seat = jnp.bitwise_and(donor_row, 127).astype(F32)
    owner_f = owner.astype(F32)
    columns = []
    for tile in range(8):
        row = owner_f[:, tile * 128 : (tile + 1) * 128]
        columns.append(jnp.broadcast_to(row, (128, 128)).T)
    earlier = iota((128, 128), 0) < iota((128, 128), 1)
    ranks = []
    for tile in range(8):
        row = owner_f[:, tile * 128 : (tile + 1) * 128]
        total = ones_where((columns[tile] == row) & earlier)
        for before in range(tile):
            total = total + ones_where(columns[before] == row)
        ranks.append(jnp.sum(total, axis=0, keepdims=True))
    rank = jnp.concatenate(ranks, axis=1).astype(jnp.int32)
    far_z = jnp.bitwise_and(lax.shift_right_logical(owner, 3), 15)
    step_x = jnp.bitwise_and(lax.shift_right_logical(owner, 7) - x + 4, 3)
    step_core = jnp.bitwise_and(lax.shift_right_logical(owner, 2) - core + 2, 1)
    step_y = jnp.bitwise_and(owner - y + 4, 3)
    plane_step = step_x * 8 + step_core * 4 + step_y
    order = jnp.bitwise_and(far_z - z + 11 + NZ, NZ - 1)
    slot = plane_step * 32 + lax.shift_right_logical(order, 1) * 4 + rank
    odd = jnp.bitwise_and(order, 1)
    slot_even = jnp.where(odd == 0, slot, -1)
    slot_odd = jnp.where(odd == 1, slot, -1)

    for load in loads[1:4]:
        load.wait()
    upper0 = counts[0:1, :]
    upper1 = upper0 + counts[1:2, :]
    upper2 = upper1 + counts[2:3, :]
    point = iota((64, 256), 0)
    inside = (
        point < upper0,
        (point >= upper0) & (point < upper1),
        (point >= upper1) & (point < upper2),
        point >= upper2,
    )
    spans = ((0, 32), (0, 64), (0, 64), (32, 64))
    fine = fine_basis[...].T
    for v in range(5):
        values = lax.dot_general(
            fine,
            residual[v],
            (((1,), (0,)), ((), ())),
            precision=lax.Precision.HIGHEST,
            preferred_element_type=F32,
        )
        for k in range(4):
            masked[k, v] = jnp.where(inside[k], values, F32(0.0))
    loads[4].wait()
    for a in range(10):
        for k in range(4):
            low, high = spans[k]
            product = basis[a, low:high, :][None] * masked[k, :, low:high, :]
            pair[a * 5 : a * 5 + 5, k * 256 : (k + 1) * 256] = jnp.sum(product, axis=1)
    pair[50:51, :] = seat
    pair[51:64, :] = jnp.zeros((13, 1024), F32)
    pair_high, pair_low = halves(pair[...])
    nothing = jnp.zeros((64, 1024), BF16)
    spread[0] = jnp.concatenate([pair_high, nothing, pair_low, nothing], axis=0)
    spread[1] = jnp.concatenate([nothing, pair_high, nothing, pair_low], axis=0)

    for part in PARTS:
        slots = iota((256, 1024), 0) + part * 256
        rows = dot_nt(ones_where(slots == slot_even).astype(BF16), spread[0])
        rows = rows + dot_nt(ones_where(slots == slot_odd).astype(BF16), spread[1])
        rows = rows[:, :128] + rows[:, 128:]
        outbox[part * 8 : (part + 1) * 8] = rows.reshape(8, 4, 8, 128)

    pl.semaphore_wait(barrier, 39)
    loads[5].wait()

    group_pos[0] = jnp.broadcast_to(positions[...], (8, 128))

    def pos_copy(step):
        return pltpu.make_async_remote_copy(
            src_ref=group_pos.at[0],
            dst_ref=group_pos.at[step],
            send_sem=pos_send.at[step],
            recv_sem=pos_recv.at[step],
            device_id=group_peer(step),
            device_id_type=MESH,
        )

    def plane_copy(half, step):
        return pltpu.make_async_remote_copy(
            src_ref=outbox.at[step, pl.ds(half * 2, 2)],
            dst_ref=inbox.at[pl.ds(half * 2, 2), step],
            send_sem=plane_send.at[half],
            recv_sem=plane_recv.at[half],
            device_id=plane_peer(step),
            device_id_type=MESH,
        )

    for half in range(2):
        for part in PARTS:
            plane_steps(part, lambda step, half=half: plane_copy(half, step).start())
    for step in range(1, NY):
        pos_copy(step).start()
    inbox[:, 0] = outbox[0]

    for load in loads[6:8]:
        load.wait()
    own = iota((1, 128), 1)
    for f in range(4):
        offset = offsets[f : f + 1, :]
        there = block * 128 + own + offset
        good = (offset != 0) & (there >= 0) & (there < 65536)
        near = own + offset
        beyond = jnp.where(near < 0, near + 256, near)
        wanted = jnp.where(good, beyond, -1)
        for half in range(2):
            source = iota((128, 128), 0) + half * 128
            chooser[half * 128 : half * 128 + 128, f * 128 : f * 128 + 128] = ones_where(
                source == wanted
            ).astype(BF16)
    row_v = lax.shift_right_logical(iota((80, 64), 0), 4)
    col = iota((80, 64), 1)
    fifth = jnp.zeros((80, 64), jnp.int32)
    for b in range(1, 10):
        fifth = fifth + jnp.where(col >= b * 5, 1, 0)
    same = (col - fifth * 5 == row_v) & (col < 50)
    take_a = ones_where(
        jnp.bitwise_and(iota((80, 10), 0), 15) == iota((80, 10), 1)
    ).astype(BF16)
    b_low = iota((10, 64), 0) * 5
    b_col = iota((10, 64), 1)
    take_b = ones_where((b_col >= b_low) & (b_col < b_low + 5)).astype(BF16)
    for f in range(4):
        for n, part in enumerate(halves(lift[:, f, :])):
            wide = dot_nn(dot_nn(take_a, part).astype(BF16), take_b)
            wide = jnp.where(same, wide, F32(0.0)).astype(BF16)
            lift_rows[f, n * 80 : n * 80 + 80, :] = jnp.concatenate([wide, wide], axis=1)
    for step in range(1, NY):
        pos_copy(step).wait_recv()
    place = iota((128, 128), 0) + block * 128
    for step in range(NY):
        seats_to_pos[:, step * 128 : step * 128 + 128] = ones_where(
            place == group_pos[step, 0:1, :]
        ).astype(BF16)

    def wait_plane(half, sems):
        whole = inbox.at[pl.ds(half * 2, 2), pl.ds(1, NP - 1)]
        pltpu.make_async_copy(whole, whole, sems.at[half]).wait()

    in_pair = jnp.bitwise_and(lax.shift_right_logical(iota((128, 256), 1), 2), 1)
    cell = iota((128, 256), 0).astype(F32)

    def gather(quarter):
        turned = inbox[quarter].reshape(256, 128).T
        high, low = halves(turned)
        for h in range(2):
            left = jnp.concatenate(
                [high[h * 64 : h * 64 + 64], low[h * 64 : h * 64 + 64]], axis=0
            )
            hit = cell == turned[h * 64 + 50 : h * 64 + 51, :]
            right = jnp.concatenate(
                [
                    ones_where(hit & (in_pair == 0)).astype(BF16),
                    ones_where(hit & (in_pair == 1)).astype(BF16),
                ],
                axis=0,
            )
            both = dot_nt(left, right)
            both = both[:64] + both[64:]
            for n in range(2):
                chunks[quarter * 4 + n * 2 + h] = both[:, n * 128 : n * 128 + 128]

    def chunk_of(relative):
        return (relative + 11) % 16

    def hop_copy(hop, n):
        step, relative = HOPS[hop][n]
        return pltpu.make_async_remote_copy(
            src_ref=chunks.at[chunk_of(relative), pl.ds(0, ROWS)],
            dst_ref=hop_in.at[hop, n],
            send_sem=hop_send.at[hop, n],
            recv_sem=hop_recv.at[hop, n],
            device_id=ring_peer(step % NZ),
            device_id_type=MESH,
        )

    def add_up(hop, members, relative):
        for n in members:
            hop_copy(hop, n).wait_recv()
        added = hop_in[hop, members[0]]
        for n in members[1:]:
            added = added + hop_in[hop, n]
        chunks[chunk_of(relative), 0:ROWS, :] += added

    wait_plane(0, plane_recv)
    gather(0)
    for hop, n in ((0, 0), (0, 1), (1, 0)):
        hop_copy(hop, n).start()
    gather(1)
    for hop, n in ((0, 2), (1, 2), (1, 3)):
        hop_copy(hop, n).start()
    wait_plane(1, plane_recv)
    gather(3)
    hop_copy(1, 1).start()
    add_up(0, (0, 1), 6)
    hop_copy(1, 4).start()
    add_up(0, (2,), -6)
    hop_copy(1, 5).start()
    gather(2)
    for n in range(4):
        hop_copy(2, n).start()
    add_up(1, (0, 1, 4), 3)
    hop_copy(2, 4).start()
    add_up(1, (2, 3, 5), -3)
    hop_copy(2, 5).start()
    def group_copy(step):
        return pltpu.make_async_remote_copy(
            src_ref=group.at[0],
            dst_ref=group.at[step],
            send_sem=group_send.at[step],
            recv_sem=group_recv.at[step],
            device_id=group_peer(step),
            device_id_type=MESH,
        )

    add_up(2, (0, 1, 2, 3, 4, 5), 0)
    group[0] = chunks[chunk_of(0), 0:ROWS, :]
    for step in (2, 1, 3):
        group_copy(step).start()
    for load in loads[8:]:
        load.wait()
    for step in (1, 3, 2):
        group_copy(step).wait_recv()
    blank = jnp.zeros((14, 128), F32)
    wide = jnp.concatenate(
        [jnp.concatenate([group[step], blank], axis=0) for step in range(NY)], axis=1
    )
    high, low = halves(wide)
    coarse = dot_nt(jnp.concatenate([high, low], axis=0), seats_to_pos[...])
    coarse = (coarse[:64] + coarse[64:])[:50]
    coarse_out[...] = coarse

    def apply_inverse(field):
        return jnp.sum(inverse[...] * field[None], axis=1)

    def halo_copy(it, up):
        return pltpu.make_async_remote_copy(
            src_ref=(ends_high if up else ends_low).at[it],
            dst_ref=(halo_low if up else halo_high).at[it],
            send_sem=halo_send.at[it, 0 if up else 1],
            recv_sem=halo_recv.at[it, 0 if up else 1],
            device_id=line_peer(1 if up else 511),
            device_id_type=MESH,
        )

    lane_part = lax.shift_right_logical(iota((16, 128), 1), 5)

    def packed(rows, from_part):
        total = jnp.zeros((16, 128), F32)
        for g in range(4):
            shift = (g - from_part) % 4 * 32
            group_rows = rows[g * 16 : g * 16 + 16]
            turned = pltpu.roll(group_rows, shift, 1) if shift else group_rows
            total = jnp.where(lane_part == g, turned, total)
        return total

    def unpacked(low_ends, high_ends):
        parts = []
        for g in range(4):
            low_shift = (3 - g) % 4 * 32
            high_shift = (4 - g) % 4 * 32
            low_rows = pltpu.roll(low_ends, low_shift, 1) if low_shift else low_ends
            high_rows = pltpu.roll(high_ends, high_shift, 1) if high_shift else high_ends
            parts.append(jnp.where(lane_part == 3, low_rows, jnp.where(lane_part == 0, high_rows, F32(0.0))))
        return jnp.concatenate(parts, axis=0)

    field = apply_inverse(coarse)
    tail = jnp.zeros((14, 128), F32)
    for it in range(2):
        whole = jnp.concatenate([field, tail], axis=0)
        ends_high[it] = packed(whole, 3)
        ends_low[it] = packed(whole, 0)
        halo_copy(it, True).start()
        halo_copy(it, False).start()
        halo_copy(it, True).wait_recv()
        halo_copy(it, False).wait_recv()
        wide = jnp.concatenate([whole, unpacked(halo_low[it], halo_high[it])], axis=1)
        high, low = halves(wide)
        picked = dot_nn(jnp.concatenate([high, low], axis=0), chooser[...]).astype(BF16)
        lifted = []
        for f in range(4):
            both = dot_nn(lift_rows[f], picked[:, f * 128 : f * 128 + 128])
            lifted.append(both[:80] + both[80:])
        for w in range(5):
            total = jnp.zeros((16, 128), F32)
            for f in range(4):
                for v in range(5):
                    total = total + lifted[f][v * 16 : v * 16 + 16] * jacobian[w, v, f : f + 1, :]
            coupling[pl.ds(w, 10, stride=5), :] = total[:10]
        field = apply_inverse(coarse - coupling[0:50, :])
    correction_out[...] = field

    for half in range(2):
        wait_plane(half, plane_send)
    for hop in range(3):
        for n in range(len(HOPS[hop])):
            hop_copy(hop, n).wait_send()
    for step in range(1, NY):
        pos_copy(step).wait_send()
        group_copy(step).wait_send()
    for it in range(2):
        halo_copy(it, True).wait_send()
        halo_copy(it, False).wait_send()


def per_device(
    fine_residual,
    fine_basis,
    coarse_basis,
    donor_cells,
    point_counts,
    solver_pos,
    block_inverse,
    face_jacobian,
    face_lift,
    face_offset,
):
    vmem = pl.BlockSpec(memory_space=pltpu.VMEM)
    hbm = pl.BlockSpec(memory_space=pl.ANY)
    dma = pltpu.SemaphoreType.DMA
    return pl.pallas_call(
        kernel,
        out_shape=(
            jax.ShapeDtypeStruct((50, 128), F32),
            jax.ShapeDtypeStruct((50, 128), F32),
        ),
        in_specs=[hbm] * 10,
        out_specs=(vmem, vmem),
        scratch_shapes=[
            pltpu.VMEM((5, 35, 256), F32),
            pltpu.VMEM((35, 64), F32),
            pltpu.VMEM((10, 64, 256), F32),
            pltpu.VMEM((4, 256), jnp.int32),
            pltpu.VMEM((4, 256), jnp.int32),
            pltpu.VMEM((1, 128), jnp.int32),
            pltpu.VMEM((50, 50, 128), F32),
            pltpu.VMEM((5, 5, 4, 128), F32),
            pltpu.VMEM((10, 4, 10), F32),
            pltpu.VMEM((4, 128), jnp.int32),
            pltpu.VMEM((4, 5, 64, 256), F32),
            pltpu.VMEM((64, 1024), F32),
            pltpu.VMEM((2, 256, 1024), BF16),
            pltpu.VMEM((NP, 4, 8, 128), F32),
            pltpu.VMEM((4, NP, 8, 128), F32),
            pltpu.VMEM((NZ, 64, 128), F32),
            pltpu.VMEM((3, 6, ROWS, 128), F32),
            pltpu.VMEM((NY, ROWS, 128), F32),
            pltpu.VMEM((NY, 8, 128), jnp.int32),
            pltpu.VMEM((128, 512), BF16),
            pltpu.VMEM((256, 512), BF16),
            pltpu.VMEM((4, 160, 128), BF16),
            pltpu.VMEM((2, 16, 128), F32),
            pltpu.VMEM((2, 16, 128), F32),
            pltpu.VMEM((2, 16, 128), F32),
            pltpu.VMEM((2, 16, 128), F32),
            pltpu.VMEM((64, 128), F32),
            dma((10,)),
            dma((2,)),
            dma((2,)),
            dma((3, 6)),
            dma((3, 6)),
            dma((NY,)),
            dma((NY,)),
            dma((NY,)),
            dma((NY,)),
            dma((2, 2)),
            dma((2, 2)),
        ],
        compiler_params=pltpu.CompilerParams(
            collective_id=0, has_side_effects=True
        ),
    )(
        fine_residual.transpose(1, 0, 2),
        fine_basis.T,
        coarse_basis.transpose(1, 0, 2),
        donor_cells.T,
        point_counts.T,
        solver_pos.reshape(1, 128),
        block_inverse,
        face_jacobian.transpose(1, 2, 0, 3),
        face_lift.transpose(1, 0, 2),
        face_offset,
    )


def solution(mesh):
    in_specs = (
        P(None, None, ("dom", "sub")),
        P(),
        P(None, None, ("dom", "sub")),
        P(("dom", "sub"), None),
        P(("dom", "sub"), None),
        P(("dom", "sub")),
        P(None, None, ("dom", "sub")),
        P(None, None, None, ("dom", "sub")),
        P(),
        P(None, ("dom", "sub")),
    )
    out_specs = (P(None, ("dom", "sub")), P(None, ("dom", "sub")))
    return jax.shard_map(
        per_device, mesh=mesh, in_specs=in_specs, out_specs=out_specs, check_vma=False
    )
```

```python
import functools

import jax
import jax.numpy as jnp
from jax import lax
from jax.experimental import pallas as pl
from jax.experimental.pallas import tpu as pltpu
from jax.sharding import PartitionSpec as P

MESH = pl.DeviceIdType.MESH
F32 = jnp.float32
BF16 = jnp.bfloat16

NZ = 16
NP = 32
NY = 4
ROWS = 50
PARTS = (2, 1, 3, 0)
HOPS = (
    ((2, 8), (1, 7), (-1, -7)),
    ((2, 5), (1, 4), (-2, -5), (-1, -4), (3, 6), (-3, -6)),
    ((2, 2), (1, 1), (-2, -2), (-1, -1), (3, 3), (-3, -3)),
)


def halves(value):
    high = value.astype(BF16)
    return high, (value - high.astype(F32)).astype(BF16)


def dot_nt(left, right):
    return lax.dot_general(left, right, (((1,), (1,)), ((), ())), preferred_element_type=F32)


def dot_nn(left, right):
    return lax.dot_general(left, right, (((1,), (0,)), ((), ())), preferred_element_type=F32)


def ones_where(mask):
    return jnp.where(mask, F32(1.0), F32(0.0))


def iota(shape, dim):
    return lax.broadcasted_iota(jnp.int32, shape, dim)


def kernel(
    residual_hbm,
    fine_basis_hbm,
    basis_hbm,
    donors_hbm,
    counts_hbm,
    positions_hbm,
    inverse_hbm,
    jacobian_hbm,
    lift_hbm,
    offsets_hbm,
    result,
    residual,
    fine_basis,
    basis,
    donors,
    counts,
    positions,
    inverse,
    jacobian,
    lift,
    offsets,
    masked,
    pair,
    spread,
    outbox,
    inbox,
    chunks,
    hop_in,
    group,
    group_pos,
    seats_to_pos,
    chooser,
    lift_rows,
    ends_high,
    ends_low,
    halo_low,
    halo_high,
    coupling,
    load_sem,
    plane_send,
    plane_recv,
    hop_send,
    hop_recv,
    group_send,
    group_recv,
    pos_send,
    pos_recv,
    halo_send,
    halo_recv,
):
    dom = lax.axis_index("dom")
    y = lax.axis_index("sub")
    x = lax.div(dom, 32)
    z = lax.rem(lax.div(dom, 2), NZ)
    core = lax.rem(dom, 2)
    block = dom * NY + y

    def plane_peer(step):
        far_x = lax.rem(x + lax.div(step, 8), 4)
        far_core = lax.rem(core + lax.div(step, 4), 2)
        far_y = lax.rem(y + step, NY)
        return ((far_x * NZ + z) * 2 + far_core, far_y)

    def ring_peer(step):
        return ((x * NZ + lax.rem(z + step, NZ)) * 2 + core, y)

    def group_peer(step):
        return (dom, lax.rem(y + step, NY))

    def line_peer(step):
        other = lax.rem(block + step, 512)
        return (lax.div(other, NY), lax.rem(other, NY))

    loads = [
        pltpu.make_async_copy(source, target, load_sem.at[n])
        for n, (source, target) in enumerate(
            (
                (donors_hbm, donors),
                (counts_hbm, counts),
                (fine_basis_hbm, fine_basis),
                (residual_hbm, residual),
                (basis_hbm, basis),
                (positions_hbm, positions),
                (offsets_hbm, offsets),
                (lift_hbm, lift),
                (jacobian_hbm, jacobian),
                (inverse_hbm, inverse),
            )
        )
    ]
    for load in loads:
        load.start()

    barrier = pltpu.get_barrier_semaphore()

    for step in (3, 13, 2, 14, 1, 15):
        pl.semaphore_signal(barrier, inc=1, device_id=ring_peer(step), device_id_type=MESH)

    def plane_steps(part, body):
        def turned(i, carry):
            body(part * 8 + lax.rem(i, 2) * 4 + lax.rem(2 + 3 * lax.div(i, 2), NY))
            return carry

        def near(step, carry):
            body(step)
            return carry

        if part:
            lax.fori_loop(0, 8, turned, 0)
        else:
            lax.fori_loop(1, 8, near, 0)

    def greet(step):
        pl.semaphore_signal(barrier, inc=1, device_id=plane_peer(step), device_id_type=MESH)

    for part in PARTS:
        plane_steps(part, greet)
    for step in (1, 511):
        pl.semaphore_signal(barrier, inc=1, device_id=line_peer(step), device_id_type=MESH)

    loads[0].wait()
    donor_row = jnp.concatenate([donors[k : k + 1, :] for k in range(4)], axis=1)
    owner = lax.shift_right_logical(donor_row, 7)
    seat = jnp.bitwise_and(donor_row, 127).astype(F32)
    owner_f = owner.astype(F32)
    columns = []
    for tile in range(8):
        row = owner_f[:, tile * 128 : (tile + 1) * 128]
        columns.append(jnp.broadcast_to(row, (128, 128)).T)
    earlier = iota((128, 128), 0) < iota((128, 128), 1)
    ranks = []
    for tile in range(8):
        row = owner_f[:, tile * 128 : (tile + 1) * 128]
        total = ones_where((columns[tile] == row) & earlier)
        for before in range(tile):
            total = total + ones_where(columns[before] == row)
        ranks.append(jnp.sum(total, axis=0, keepdims=True))
    rank = jnp.concatenate(ranks, axis=1).astype(jnp.int32)
    far_z = jnp.bitwise_and(lax.shift_right_logical(owner, 3), 15)
    step_x = jnp.bitwise_and(lax.shift_right_logical(owner, 7) - x + 4, 3)
    step_core = jnp.bitwise_and(lax.shift_right_logical(owner, 2) - core + 2, 1)
    step_y = jnp.bitwise_and(owner - y + 4, 3)
    plane_step = step_x * 8 + step_core * 4 + step_y
    order = jnp.bitwise_and(far_z - z + 11 + NZ, NZ - 1)
    slot = plane_step * 32 + lax.shift_right_logical(order, 1) * 4 + rank
    odd = jnp.bitwise_and(order, 1)
    slot_even = jnp.where(odd == 0, slot, -1)
    slot_odd = jnp.where(odd == 1, slot, -1)

    for load in loads[1:4]:
        load.wait()
    upper0 = counts[0:1, :]
    upper1 = upper0 + counts[1:2, :]
    upper2 = upper1 + counts[2:3, :]
    point = iota((64, 256), 0)
    inside = (
        point < upper0,
        (point >= upper0) & (point < upper1),
        (point >= upper1) & (point < upper2),
        point >= upper2,
    )
    spans = ((0, 32), (0, 64), (0, 64), (32, 64))
    fine = fine_basis[...].T
    for v in range(5):
        values = lax.dot_general(
            fine,
            residual[v],
            (((1,), (0,)), ((), ())),
            precision=lax.Precision.HIGHEST,
            preferred_element_type=F32,
        )
        for k in range(4):
            masked[k, v] = jnp.where(inside[k], values, F32(0.0))
    loads[4].wait()
    for a in range(10):
        for k in range(4):
            low, high = spans[k]
            product = basis[a, low:high, :][None] * masked[k, :, low:high, :]
            pair[a * 5 : a * 5 + 5, k * 256 : (k + 1) * 256] = jnp.sum(product, axis=1)
    pair[50:51, :] = seat
    pair[51:64, :] = jnp.zeros((13, 1024), F32)
    pair_high, pair_low = halves(pair[...])
    nothing = jnp.zeros((64, 1024), BF16)
    spread[0] = jnp.concatenate([pair_high, nothing, pair_low, nothing], axis=0)
    spread[1] = jnp.concatenate([nothing, pair_high, nothing, pair_low], axis=0)

    for part in PARTS:
        slots = iota((256, 1024), 0) + part * 256
        rows = dot_nt(ones_where(slots == slot_even).astype(BF16), spread[0])
        rows = rows + dot_nt(ones_where(slots == slot_odd).astype(BF16), spread[1])
        rows = rows[:, :128] + rows[:, 128:]
        outbox[part * 8 : (part + 1) * 8] = rows.reshape(8, 4, 8, 128)

    pl.semaphore_wait(barrier, 39)
    loads[5].wait()

    group_pos[0] = jnp.broadcast_to(positions[...], (8, 128))

    def pos_copy(step):
        return pltpu.make_async_remote_copy(
            src_ref=group_pos.at[0],
            dst_ref=group_pos.at[step],
            send_sem=pos_send.at[step],
            recv_sem=pos_recv.at[step],
            device_id=group_peer(step),
            device_id_type=MESH,
        )

    def plane_copy(half, step):
        return pltpu.make_async_remote_copy(
            src_ref=outbox.at[step, pl.ds(half * 2, 2)],
            dst_ref=inbox.at[pl.ds(half * 2, 2), step],
            send_sem=plane_send.at[half],
            recv_sem=plane_recv.at[half],
            device_id=plane_peer(step),
            device_id_type=MESH,
        )

    for half in range(2):
        for part in PARTS:
            plane_steps(part, lambda step, half=half: plane_copy(half, step).start())
    for step in range(1, NY):
        pos_copy(step).start()
    inbox[:, 0] = outbox[0]

    for load in loads[6:8]:
        load.wait()
    own = iota((1, 128), 1)
    for f in range(4):
        offset = offsets[f : f + 1, :]
        there = block * 128 + own + offset
        good = (offset != 0) & (there >= 0) & (there < 65536)
        near = own + offset
        beyond = jnp.where(near < 0, near + 256, near)
        wanted = jnp.where(good, beyond, -1)
        for half in range(2):
            source = iota((128, 128), 0) + half * 128
            chooser[half * 128 : half * 128 + 128, f * 128 : f * 128 + 128] = ones_where(
                source == wanted
            ).astype(BF16)
    row_v = lax.shift_right_logical(iota((80, 64), 0), 4)
    col = iota((80, 64), 1)
    fifth = jnp.zeros((80, 64), jnp.int32)
    for b in range(1, 10):
        fifth = fifth + jnp.where(col >= b * 5, 1, 0)
    same = (col - fifth * 5 == row_v) & (col < 50)
    take_a = ones_where(
        jnp.bitwise_and(iota((80, 10), 0), 15) == iota((80, 10), 1)
    ).astype(BF16)
    b_low = iota((10, 64), 0) * 5
    b_col = iota((10, 64), 1)
    take_b = ones_where((b_col >= b_low) & (b_col < b_low + 5)).astype(BF16)
    for f in range(4):
        for n, part in enumerate(halves(lift[:, f, :])):
            wide = dot_nn(dot_nn(take_a, part).astype(BF16), take_b)
            wide = jnp.where(same, wide, F32(0.0)).astype(BF16)
            lift_rows[f, n * 80 : n * 80 + 80, :] = jnp.concatenate([wide, wide], axis=1)
    for step in range(1, NY):
        pos_copy(step).wait_recv()
    place = iota((128, 128), 0) + block * 128
    for step in range(NY):
        seats_to_pos[:, step * 128 : step * 128 + 128] = ones_where(
            place == group_pos[step, 0:1, :]
        ).astype(BF16)

    def wait_plane(half, sems):
        whole = inbox.at[pl.ds(half * 2, 2), pl.ds(1, NP - 1)]
        pltpu.make_async_copy(whole, whole, sems.at[half]).wait()

    in_pair = jnp.bitwise_and(lax.shift_right_logical(iota((128, 256), 1), 2), 1)
    cell = iota((128, 256), 0).astype(F32)

    def gather(quarter):
        turned = inbox[quarter].reshape(256, 128).T
        high, low = halves(turned)
        for h in range(2):
            left = jnp.concatenate(
                [high[h * 64 : h * 64 + 64], low[h * 64 : h * 64 + 64]], axis=0
            )
            hit = cell == turned[h * 64 + 50 : h * 64 + 51, :]
            right = jnp.concatenate(
                [
                    ones_where(hit & (in_pair == 0)).astype(BF16),
                    ones_where(hit & (in_pair == 1)).astype(BF16),
                ],
                axis=0,
            )
            both = dot_nt(left, right)
            both = both[:64] + both[64:]
            for n in range(2):
                chunks[quarter * 4 + n * 2 + h] = both[:, n * 128 : n * 128 + 128]

    def chunk_of(relative):
        return (relative + 11) % 16

    def hop_copy(hop, n):
        step, relative = HOPS[hop][n]
        return pltpu.make_async_remote_copy(
            src_ref=chunks.at[chunk_of(relative), pl.ds(0, ROWS)],
            dst_ref=hop_in.at[hop, n],
            send_sem=hop_send.at[hop, n],
            recv_sem=hop_recv.at[hop, n],
            device_id=ring_peer(step % NZ),
            device_id_type=MESH,
        )

    def add_up(hop, members, relative):
        for n in members:
            hop_copy(hop, n).wait_recv()
        added = hop_in[hop, members[0]]
        for n in members[1:]:
            added = added + hop_in[hop, n]
        chunks[chunk_of(relative), 0:ROWS, :] += added

    wait_plane(0, plane_recv)
    gather(0)
    for hop, n in ((0, 0), (0, 1), (1, 0)):
        hop_copy(hop, n).start()
    gather(1)
    for hop, n in ((0, 2), (1, 2), (1, 3)):
        hop_copy(hop, n).start()
    wait_plane(1, plane_recv)
    gather(3)
    hop_copy(1, 1).start()
    add_up(0, (0, 1), 6)
    hop_copy(1, 4).start()
    add_up(0, (2,), -6)
    hop_copy(1, 5).start()
    gather(2)
    for n in range(4):
        hop_copy(2, n).start()
    add_up(1, (0, 1, 4), 3)
    hop_copy(2, 4).start()
    add_up(1, (2, 3, 5), -3)
    hop_copy(2, 5).start()
    def group_copy(step):
        return pltpu.make_async_remote_copy(
            src_ref=group.at[0],
            dst_ref=group.at[step],
            send_sem=group_send.at[step],
            recv_sem=group_recv.at[step],
            device_id=group_peer(step),
            device_id_type=MESH,
        )

    add_up(2, (0, 1, 2, 3, 4, 5), 0)
    group[0] = chunks[chunk_of(0), 0:ROWS, :]
    for step in (2, 1, 3):
        group_copy(step).start()
    for load in loads[8:]:
        load.wait()
    for step in (1, 3, 2):
        group_copy(step).wait_recv()
    blank = jnp.zeros((14, 128), F32)
    wide = jnp.concatenate(
        [jnp.concatenate([group[step], blank], axis=0) for step in range(NY)], axis=1
    )
    high, low = halves(wide)
    coarse = dot_nt(jnp.concatenate([high, low], axis=0), seats_to_pos[...])
    coarse = (coarse[:64] + coarse[64:])[:50]
    result[0, 0:50, :] = coarse

    def apply_inverse(field):
        return jnp.sum(inverse[...] * field[None], axis=1)

    def halo_copy(it, up):
        return pltpu.make_async_remote_copy(
            src_ref=(ends_high if up else ends_low).at[it],
            dst_ref=(halo_low if up else halo_high).at[it],
            send_sem=halo_send.at[it, 0 if up else 1],
            recv_sem=halo_recv.at[it, 0 if up else 1],
            device_id=line_peer(1 if up else 511),
            device_id_type=MESH,
        )

    lane_part = lax.shift_right_logical(iota((16, 128), 1), 5)

    def packed(rows, from_part):
        total = jnp.zeros((16, 128), F32)
        for g in range(4):
            shift = (g - from_part) % 4 * 32
            group_rows = rows[g * 16 : g * 16 + 16]
            turned = pltpu.roll(group_rows, shift, 1) if shift else group_rows
            total = jnp.where(lane_part == g, turned, total)
        return total

    def unpacked(low_ends, high_ends):
        parts = []
        for g in range(4):
            low_shift = (3 - g) % 4 * 32
            high_shift = (4 - g) % 4 * 32
            low_rows = pltpu.roll(low_ends, low_shift, 1) if low_shift else low_ends
            high_rows = pltpu.roll(high_ends, high_shift, 1) if high_shift else high_ends
            parts.append(jnp.where(lane_part == 3, low_rows, jnp.where(lane_part == 0, high_rows, F32(0.0))))
        return jnp.concatenate(parts, axis=0)

    tail = jnp.zeros((14, 128), F32)
    coupling[0:50, :] = jnp.zeros((50, 128), F32)

    def sweep(it, carry):
        field = apply_inverse(result[0, 0:50, :] - coupling[0:50, :])
        result[1, 0:50, :] = field

        @pl.when(it < 2)
        def _():
            whole = jnp.concatenate([field, tail], axis=0)
            ends_high[it] = packed(whole, 3)
            ends_low[it] = packed(whole, 0)
            halo_copy(it, True).start()
            halo_copy(it, False).start()
            halo_copy(it, True).wait_recv()
            halo_copy(it, False).wait_recv()
            wide = jnp.concatenate([whole, unpacked(halo_low[it], halo_high[it])], axis=1)
            high, low = halves(wide)
            picked = dot_nn(jnp.concatenate([high, low], axis=0), chooser[...]).astype(BF16)
            lifted = []
            for f in range(4):
                both = dot_nn(lift_rows[f], picked[:, f * 128 : f * 128 + 128])
                lifted.append(both[:80] + both[80:])
            for w in range(5):
                total = jnp.zeros((16, 128), F32)
                for f in range(4):
                    for v in range(5):
                        total = total + lifted[f][v * 16 : v * 16 + 16] * jacobian[w, v, f : f + 1, :]
                coupling[pl.ds(w, 10, stride=5), :] = total[:10]

        return carry

    lax.fori_loop(0, 3, sweep, 0)

    for half in range(2):
        wait_plane(half, plane_send)
    for hop in range(3):
        for n in range(len(HOPS[hop])):
            hop_copy(hop, n).wait_send()
    for step in range(1, NY):
        pos_copy(step).wait_send()
        group_copy(step).wait_send()
    for it in range(2):
        halo_copy(it, True).wait_send()
        halo_copy(it, False).wait_send()


def per_device(
    fine_residual,
    fine_basis,
    coarse_basis,
    donor_cells,
    point_counts,
    solver_pos,
    block_inverse,
    face_jacobian,
    face_lift,
    face_offset,
):
    vmem = pl.BlockSpec(memory_space=pltpu.VMEM)
    hbm = pl.BlockSpec(memory_space=pl.ANY)
    dma = pltpu.SemaphoreType.DMA
    result = pl.pallas_call(
        kernel,
        out_shape=jax.ShapeDtypeStruct((2, 56, 128), F32),
        in_specs=[hbm] * 10,
        out_specs=vmem,
        scratch_shapes=[
            pltpu.VMEM((5, 35, 256), F32),
            pltpu.VMEM((35, 64), F32),
            pltpu.VMEM((10, 64, 256), F32),
            pltpu.VMEM((4, 256), jnp.int32),
            pltpu.VMEM((4, 256), jnp.int32),
            pltpu.VMEM((1, 128), jnp.int32),
            pltpu.VMEM((50, 50, 128), F32),
            pltpu.VMEM((5, 5, 4, 128), F32),
            pltpu.VMEM((10, 4, 10), F32),
            pltpu.VMEM((4, 128), jnp.int32),
            pltpu.VMEM((4, 5, 64, 256), F32),
            pltpu.VMEM((64, 1024), F32),
            pltpu.VMEM((2, 256, 1024), BF16),
            pltpu.VMEM((NP, 4, 8, 128), F32),
            pltpu.VMEM((4, NP, 8, 128), F32),
            pltpu.VMEM((NZ, 64, 128), F32),
            pltpu.VMEM((3, 6, ROWS, 128), F32),
            pltpu.VMEM((NY, ROWS, 128), F32),
            pltpu.VMEM((NY, 8, 128), jnp.int32),
            pltpu.VMEM((128, 512), BF16),
            pltpu.VMEM((256, 512), BF16),
            pltpu.VMEM((4, 160, 128), BF16),
            pltpu.VMEM((2, 16, 128), F32),
            pltpu.VMEM((2, 16, 128), F32),
            pltpu.VMEM((2, 16, 128), F32),
            pltpu.VMEM((2, 16, 128), F32),
            pltpu.VMEM((64, 128), F32),
            dma((10,)),
            dma((2,)),
            dma((2,)),
            dma((3, 6)),
            dma((3, 6)),
            dma((NY,)),
            dma((NY,)),
            dma((NY,)),
            dma((NY,)),
            dma((2, 2)),
            dma((2, 2)),
        ],
        compiler_params=pltpu.CompilerParams(
            collective_id=0, has_side_effects=True
        ),
    )(
        fine_residual.transpose(1, 0, 2),
        fine_basis.T,
        coarse_basis.transpose(1, 0, 2),
        donor_cells.T,
        point_counts.T,
        solver_pos.reshape(1, 128),
        block_inverse,
        face_jacobian.transpose(1, 2, 0, 3),
        face_lift.transpose(1, 0, 2),
        face_offset,
    )
    return result[0, :50], result[1, :50]


def solution(mesh):
    in_specs = (
        P(None, None, ("dom", "sub")),
        P(),
        P(None, None, ("dom", "sub")),
        P(("dom", "sub"), None),
        P(("dom", "sub"), None),
        P(("dom", "sub")),
        P(None, None, ("dom", "sub")),
        P(None, None, None, ("dom", "sub")),
        P(),
        P(None, ("dom", "sub")),
    )
    out_specs = (P(None, ("dom", "sub")), P(None, ("dom", "sub")))
    return jax.shard_map(
        per_device, mesh=mesh, in_specs=in_specs, out_specs=out_specs, check_vma=False
    )
```

```python
import functools

import jax
import jax.numpy as jnp
from jax import lax
from jax.experimental import pallas as pl
from jax.experimental.pallas import tpu as pltpu
from jax.sharding import PartitionSpec as P

MESH = pl.DeviceIdType.MESH
F32 = jnp.float32
BF16 = jnp.bfloat16

NZ = 16
NP = 32
NY = 4
ROWS = 50
PARTS = (2, 1, 3, 0)
HOPS = (
    ((2, 8), (1, 7), (-1, -7)),
    ((2, 5), (1, 4), (-2, -5), (-1, -4), (3, 6), (-3, -6)),
    ((2, 2), (1, 1), (-2, -2), (-1, -1), (3, 3), (-3, -3)),
)


def halves(value):
    high = value.astype(BF16)
    return high, (value - high.astype(F32)).astype(BF16)


def dot_nt(left, right):
    return lax.dot_general(left, right, (((1,), (1,)), ((), ())), preferred_element_type=F32)


def dot_nn(left, right):
    return lax.dot_general(left, right, (((1,), (0,)), ((), ())), preferred_element_type=F32)


def ones_where(mask):
    return jnp.where(mask, F32(1.0), F32(0.0))


def iota(shape, dim):
    return lax.broadcasted_iota(jnp.int32, shape, dim)


def kernel(
    residual_hbm,
    fine_basis_hbm,
    basis_hbm,
    donors_hbm,
    counts_hbm,
    positions_hbm,
    inverse_hbm,
    jacobian_hbm,
    lift_hbm,
    offsets_hbm,
    result,
    residual,
    fine_basis,
    basis,
    donors,
    counts,
    positions,
    inverse,
    jacobian,
    lift,
    offsets,
    masked,
    pair,
    spread,
    outbox,
    inbox,
    chunks,
    hop_in,
    group,
    group_pos,
    seats_to_pos,
    chooser,
    lift_rows,
    ends_high,
    ends_low,
    halo_low,
    halo_high,
    coupling,
    load_sem,
    plane_send,
    plane_recv,
    hop_send,
    hop_recv,
    group_send,
    group_recv,
    pos_send,
    pos_recv,
    halo_send,
    halo_recv,
):
    dom = lax.axis_index("dom")
    y = lax.axis_index("sub")
    x = lax.div(dom, 32)
    z = lax.rem(lax.div(dom, 2), NZ)
    core = lax.rem(dom, 2)
    block = dom * NY + y

    def plane_peer(step):
        far_x = lax.rem(x + lax.div(step, 8), 4)
        far_core = lax.rem(core + lax.div(step, 4), 2)
        far_y = lax.rem(y + step, NY)
        return ((far_x * NZ + z) * 2 + far_core, far_y)

    def ring_peer(step):
        return ((x * NZ + lax.rem(z + step, NZ)) * 2 + core, y)

    def group_peer(step):
        return (dom, lax.rem(y + step, NY))

    def line_peer(step):
        other = lax.rem(block + step, 512)
        return (lax.div(other, NY), lax.rem(other, NY))

    loads = [
        pltpu.make_async_copy(source, target, load_sem.at[n])
        for n, (source, target) in enumerate(
            (
                (donors_hbm, donors),
                (counts_hbm, counts),
                (fine_basis_hbm, fine_basis),
                (residual_hbm, residual),
                (basis_hbm, basis),
                (positions_hbm, positions),
                (offsets_hbm, offsets),
                (lift_hbm, lift),
                (jacobian_hbm, jacobian),
                (inverse_hbm, inverse),
            )
        )
    ]
    for load in loads:
        load.start()

    barrier = pltpu.get_barrier_semaphore()

    for step in (3, 13, 2, 14, 1, 15):
        pl.semaphore_signal(barrier, inc=1, device_id=ring_peer(step), device_id_type=MESH)

    def plane_steps(part, body):
        def turned(i, carry):
            body(part * 8 + lax.rem(i, 2) * 4 + lax.rem(2 + 3 * lax.div(i, 2), NY))
            return carry

        def near(step, carry):
            body(step)
            return carry

        if part:
            lax.fori_loop(0, 8, turned, 0)
        else:
            lax.fori_loop(1, 8, near, 0)

    def greet(step):
        pl.semaphore_signal(barrier, inc=1, device_id=plane_peer(step), device_id_type=MESH)

    for part in PARTS:
        plane_steps(part, greet)
    for step in (1, 511):
        pl.semaphore_signal(barrier, inc=1, device_id=line_peer(step), device_id_type=MESH)

    loads[0].wait()
    donor_row = jnp.concatenate([donors[k : k + 1, :] for k in range(4)], axis=1)
    owner = lax.shift_right_logical(donor_row, 7)
    seat = jnp.bitwise_and(donor_row, 127).astype(F32)
    owner_f = owner.astype(F32)
    columns = []
    for tile in range(8):
        row = owner_f[:, tile * 128 : (tile + 1) * 128]
        columns.append(jnp.broadcast_to(row, (128, 128)).T)
    earlier = iota((128, 128), 0) < iota((128, 128), 1)
    ranks = []
    for tile in range(8):
        row = owner_f[:, tile * 128 : (tile + 1) * 128]
        total = ones_where((columns[tile] == row) & earlier)
        for before in range(tile):
            total = total + ones_where(columns[before] == row)
        ranks.append(jnp.sum(total, axis=0, keepdims=True))
    rank = jnp.concatenate(ranks, axis=1).astype(jnp.int32)
    far_z = jnp.bitwise_and(lax.shift_right_logical(owner, 3), 15)
    step_x = jnp.bitwise_and(lax.shift_right_logical(owner, 7) - x + 4, 3)
    step_core = jnp.bitwise_and(lax.shift_right_logical(owner, 2) - core + 2, 1)
    step_y = jnp.bitwise_and(owner - y + 4, 3)
    plane_step = step_x * 8 + step_core * 4 + step_y
    order = jnp.bitwise_and(far_z - z + 11 + NZ, NZ - 1)
    slot = plane_step * 32 + lax.shift_right_logical(order, 1) * 4 + rank
    odd = jnp.bitwise_and(order, 1)
    slot_even = jnp.where(odd == 0, slot, -1)
    slot_odd = jnp.where(odd == 1, slot, -1)

    for load in loads[1:4]:
        load.wait()
    upper0 = counts[0:1, :]
    upper1 = upper0 + counts[1:2, :]
    upper2 = upper1 + counts[2:3, :]
    point = iota((64, 256), 0)
    inside = (
        point < upper0,
        (point >= upper0) & (point < upper1),
        (point >= upper1) & (point < upper2),
        point >= upper2,
    )
    spans = ((0, 32), (0, 64), (0, 64), (32, 64))
    fine = fine_basis[...].T
    for v in range(5):
        values = lax.dot_general(
            fine,
            residual[v],
            (((1,), (0,)), ((), ())),
            precision=lax.Precision.HIGHEST,
            preferred_element_type=F32,
        )
        for k in range(4):
            masked[k, v] = jnp.where(inside[k], values, F32(0.0))
    loads[4].wait()
    for a in range(10):
        for k in range(4):
            low, high = spans[k]
            product = basis[a, low:high, :][None] * masked[k, :, low:high, :]
            pair[a * 5 : a * 5 + 5, k * 256 : (k + 1) * 256] = jnp.sum(product, axis=1)
    pair[50:51, :] = seat
    pair[51:64, :] = jnp.zeros((13, 1024), F32)
    pair_high, pair_low = halves(pair[...])
    nothing = jnp.zeros((64, 1024), BF16)
    spread[0] = jnp.concatenate([pair_high, nothing, pair_low, nothing], axis=0)
    spread[1] = jnp.concatenate([nothing, pair_high, nothing, pair_low], axis=0)

    for part in PARTS:
        slots = iota((256, 1024), 0) + part * 256
        rows = dot_nt(ones_where(slots == slot_even).astype(BF16), spread[0])
        rows = rows + dot_nt(ones_where(slots == slot_odd).astype(BF16), spread[1])
        rows = rows[:, :128] + rows[:, 128:]
        outbox[part * 8 : (part + 1) * 8] = rows.reshape(8, 4, 8, 128)

    pl.semaphore_wait(barrier, 39)
    loads[5].wait()

    group_pos[0] = jnp.broadcast_to(positions[...], (8, 128))

    def pos_copy(step):
        return pltpu.make_async_remote_copy(
            src_ref=group_pos.at[0],
            dst_ref=group_pos.at[step],
            send_sem=pos_send.at[step],
            recv_sem=pos_recv.at[step],
            device_id=group_peer(step),
            device_id_type=MESH,
        )

    def plane_copy(half, step):
        return pltpu.make_async_remote_copy(
            src_ref=outbox.at[step, pl.ds(half * 2, 2)],
            dst_ref=inbox.at[pl.ds(half * 2, 2), step],
            send_sem=plane_send.at[half],
            recv_sem=plane_recv.at[half],
            device_id=plane_peer(step),
            device_id_type=MESH,
        )

    for half in range(2):
        for part in PARTS:
            plane_steps(part, lambda step, half=half: plane_copy(half, step).start())
    for step in range(1, NY):
        pos_copy(step).start()
    inbox[:, 0] = outbox[0]

    for load in loads[6:8]:
        load.wait()
    own = iota((1, 128), 1)
    for f in range(4):
        offset = offsets[f : f + 1, :]
        there = block * 128 + own + offset
        good = (offset != 0) & (there >= 0) & (there < 65536)
        near = own + offset
        beyond = jnp.where(near < 0, near + 256, near)
        wanted = jnp.where(good, beyond, -1)
        for half in range(2):
            source = iota((128, 128), 0) + half * 128
            chooser[half * 128 : half * 128 + 128, f * 128 : f * 128 + 128] = ones_where(
                source == wanted
            ).astype(BF16)
    row_v = lax.shift_right_logical(iota((80, 64), 0), 4)
    col = iota((80, 64), 1)
    fifth = jnp.zeros((80, 64), jnp.int32)
    for b in range(1, 10):
        fifth = fifth + jnp.where(col >= b * 5, 1, 0)
    same = (col - fifth * 5 == row_v) & (col < 50)
    take_a = ones_where(
        jnp.bitwise_and(iota((80, 10), 0), 15) == iota((80, 10), 1)
    ).astype(BF16)
    b_low = iota((10, 64), 0) * 5
    b_col = iota((10, 64), 1)
    take_b = ones_where((b_col >= b_low) & (b_col < b_low + 5)).astype(BF16)
    for f in range(4):
        for n, part in enumerate(halves(lift[:, f, :])):
            wide = dot_nn(dot_nn(take_a, part).astype(BF16), take_b)
            wide = jnp.where(same, wide, F32(0.0)).astype(BF16)
            lift_rows[f, n * 80 : n * 80 + 80, :] = jnp.concatenate([wide, wide], axis=1)
    def wait_plane(half, sems):
        whole = inbox.at[pl.ds(half * 2, 2), pl.ds(1, NP - 1)]
        pltpu.make_async_copy(whole, whole, sems.at[half]).wait()

    in_pair = jnp.bitwise_and(lax.shift_right_logical(iota((128, 256), 1), 2), 1)
    cell = iota((128, 256), 0).astype(F32)

    def gather(quarter):
        turned = inbox[quarter].reshape(256, 128).T
        high, low = halves(turned)
        for h in range(2):
            left = jnp.concatenate(
                [high[h * 64 : h * 64 + 64], low[h * 64 : h * 64 + 64]], axis=0
            )
            hit = cell == turned[h * 64 + 50 : h * 64 + 51, :]
            right = jnp.concatenate(
                [
                    ones_where(hit & (in_pair == 0)).astype(BF16),
                    ones_where(hit & (in_pair == 1)).astype(BF16),
                ],
                axis=0,
            )
            both = dot_nt(left, right)
            both = both[:64] + both[64:]
            for n in range(2):
                chunks[quarter * 4 + n * 2 + h] = both[:, n * 128 : n * 128 + 128]

    def chunk_of(relative):
        return (relative + 11) % 16

    def hop_copy(hop, n):
        step, relative = HOPS[hop][n]
        return pltpu.make_async_remote_copy(
            src_ref=chunks.at[chunk_of(relative), pl.ds(0, ROWS)],
            dst_ref=hop_in.at[hop, n],
            send_sem=hop_send.at[hop, n],
            recv_sem=hop_recv.at[hop, n],
            device_id=ring_peer(step % NZ),
            device_id_type=MESH,
        )

    def add_up(hop, members, relative):
        for n in members:
            hop_copy(hop, n).wait_recv()
        added = hop_in[hop, members[0]]
        for n in members[1:]:
            added = added + hop_in[hop, n]
        chunks[chunk_of(relative), 0:ROWS, :] += added

    wait_plane(0, plane_recv)
    gather(0)
    for hop, n in ((0, 0), (0, 1), (1, 0)):
        hop_copy(hop, n).start()
    gather(1)
    for hop, n in ((0, 2), (1, 2), (1, 3)):
        hop_copy(hop, n).start()
    wait_plane(1, plane_recv)
    gather(3)
    hop_copy(1, 1).start()
    for step in range(1, NY):
        pos_copy(step).wait_recv()
    place = iota((128, 128), 0) + block * 128
    for step in range(NY):
        seats_to_pos[:, step * 128 : step * 128 + 128] = ones_where(
            place == group_pos[step, 0:1, :]
        ).astype(BF16)

    add_up(0, (0, 1), 6)
    hop_copy(1, 4).start()
    add_up(0, (2,), -6)
    hop_copy(1, 5).start()
    gather(2)
    for n in range(4):
        hop_copy(2, n).start()
    add_up(1, (0, 1, 4), 3)
    hop_copy(2, 4).start()
    add_up(1, (2, 3, 5), -3)
    hop_copy(2, 5).start()
    def group_copy(step):
        return pltpu.make_async_remote_copy(
            src_ref=group.at[0],
            dst_ref=group.at[step],
            send_sem=group_send.at[step],
            recv_sem=group_recv.at[step],
            device_id=group_peer(step),
            device_id_type=MESH,
        )

    add_up(2, (0, 1, 2, 3, 4, 5), 0)
    group[0] = chunks[chunk_of(0), 0:ROWS, :]
    for step in (2, 1, 3):
        group_copy(step).start()
    for load in loads[8:]:
        load.wait()
    for step in (1, 3, 2):
        group_copy(step).wait_recv()
    blank = jnp.zeros((14, 128), F32)
    wide = jnp.concatenate(
        [jnp.concatenate([group[step], blank], axis=0) for step in range(NY)], axis=1
    )
    high, low = halves(wide)
    coarse = dot_nt(jnp.concatenate([high, low], axis=0), seats_to_pos[...])
    coarse = (coarse[:64] + coarse[64:])[:50]
    result[0, 0:50, :] = coarse

    def apply_inverse(field):
        return jnp.sum(inverse[...] * field[None], axis=1)

    def halo_copy(it, up):
        return pltpu.make_async_remote_copy(
            src_ref=(ends_high if up else ends_low).at[it],
            dst_ref=(halo_low if up else halo_high).at[it],
            send_sem=halo_send.at[it, 0 if up else 1],
            recv_sem=halo_recv.at[it, 0 if up else 1],
            device_id=line_peer(1 if up else 511),
            device_id_type=MESH,
        )

    lane_part = lax.shift_right_logical(iota((16, 128), 1), 5)

    def packed(rows, from_part):
        total = jnp.zeros((16, 128), F32)
        for g in range(4):
            shift = (g - from_part) % 4 * 32
            group_rows = rows[g * 16 : g * 16 + 16]
            turned = pltpu.roll(group_rows, shift, 1) if shift else group_rows
            total = jnp.where(lane_part == g, turned, total)
        return total

    def unpacked(low_ends, high_ends):
        parts = []
        for g in range(4):
            low_shift = (3 - g) % 4 * 32
            high_shift = (4 - g) % 4 * 32
            low_rows = pltpu.roll(low_ends, low_shift, 1) if low_shift else low_ends
            high_rows = pltpu.roll(high_ends, high_shift, 1) if high_shift else high_ends
            parts.append(jnp.where(lane_part == 3, low_rows, jnp.where(lane_part == 0, high_rows, F32(0.0))))
        return jnp.concatenate(parts, axis=0)

    tail = jnp.zeros((14, 128), F32)
    coupling[0:50, :] = jnp.zeros((50, 128), F32)

    def sweep(it, carry):
        field = apply_inverse(result[0, 0:50, :] - coupling[0:50, :])
        result[1, 0:50, :] = field

        @pl.when(it < 2)
        def _():
            whole = jnp.concatenate([field, tail], axis=0)
            ends_high[it] = packed(whole, 3)
            ends_low[it] = packed(whole, 0)
            halo_copy(it, True).start()
            halo_copy(it, False).start()
            halo_copy(it, True).wait_recv()
            halo_copy(it, False).wait_recv()
            wide = jnp.concatenate([whole, unpacked(halo_low[it], halo_high[it])], axis=1)
            high, low = halves(wide)
            picked = dot_nn(jnp.concatenate([high, low], axis=0), chooser[...]).astype(BF16)
            lifted = []
            for f in range(4):
                both = dot_nn(lift_rows[f], picked[:, f * 128 : f * 128 + 128])
                lifted.append(both[:80] + both[80:])
            for w in range(5):
                total = jnp.zeros((16, 128), F32)
                for f in range(4):
                    for v in range(5):
                        total = total + lifted[f][v * 16 : v * 16 + 16] * jacobian[w, v, f : f + 1, :]
                coupling[pl.ds(w, 10, stride=5), :] = total[:10]

        return carry

    lax.fori_loop(0, 3, sweep, 0)

    for half in range(2):
        wait_plane(half, plane_send)
    for hop in range(3):
        for n in range(len(HOPS[hop])):
            hop_copy(hop, n).wait_send()
    for step in range(1, NY):
        pos_copy(step).wait_send()
        group_copy(step).wait_send()
    for it in range(2):
        halo_copy(it, True).wait_send()
        halo_copy(it, False).wait_send()


def per_device(
    fine_residual,
    fine_basis,
    coarse_basis,
    donor_cells,
    point_counts,
    solver_pos,
    block_inverse,
    face_jacobian,
    face_lift,
    face_offset,
):
    vmem = pl.BlockSpec(memory_space=pltpu.VMEM)
    hbm = pl.BlockSpec(memory_space=pl.ANY)
    dma = pltpu.SemaphoreType.DMA
    result = pl.pallas_call(
        kernel,
        out_shape=jax.ShapeDtypeStruct((2, 56, 128), F32),
        in_specs=[hbm] * 10,
        out_specs=vmem,
        scratch_shapes=[
            pltpu.VMEM((5, 35, 256), F32),
            pltpu.VMEM((35, 64), F32),
            pltpu.VMEM((10, 64, 256), F32),
            pltpu.VMEM((4, 256), jnp.int32),
            pltpu.VMEM((4, 256), jnp.int32),
            pltpu.VMEM((1, 128), jnp.int32),
            pltpu.VMEM((50, 50, 128), F32),
            pltpu.VMEM((5, 5, 4, 128), F32),
            pltpu.VMEM((10, 4, 10), F32),
            pltpu.VMEM((4, 128), jnp.int32),
            pltpu.VMEM((4, 5, 64, 256), F32),
            pltpu.VMEM((64, 1024), F32),
            pltpu.VMEM((2, 256, 1024), BF16),
            pltpu.VMEM((NP, 4, 8, 128), F32),
            pltpu.VMEM((4, NP, 8, 128), F32),
            pltpu.VMEM((NZ, 64, 128), F32),
            pltpu.VMEM((3, 6, ROWS, 128), F32),
            pltpu.VMEM((NY, ROWS, 128), F32),
            pltpu.VMEM((NY, 8, 128), jnp.int32),
            pltpu.VMEM((128, 512), BF16),
            pltpu.VMEM((256, 512), BF16),
            pltpu.VMEM((4, 160, 128), BF16),
            pltpu.VMEM((2, 16, 128), F32),
            pltpu.VMEM((2, 16, 128), F32),
            pltpu.VMEM((2, 16, 128), F32),
            pltpu.VMEM((2, 16, 128), F32),
            pltpu.VMEM((64, 128), F32),
            dma((10,)),
            dma((2,)),
            dma((2,)),
            dma((3, 6)),
            dma((3, 6)),
            dma((NY,)),
            dma((NY,)),
            dma((NY,)),
            dma((NY,)),
            dma((2, 2)),
            dma((2, 2)),
        ],
        compiler_params=pltpu.CompilerParams(
            collective_id=0, has_side_effects=True
        ),
    )(
        fine_residual.transpose(1, 0, 2),
        fine_basis.T,
        coarse_basis.transpose(1, 0, 2),
        donor_cells.T,
        point_counts.T,
        solver_pos.reshape(1, 128),
        block_inverse,
        face_jacobian.transpose(1, 2, 0, 3),
        face_lift.transpose(1, 0, 2),
        face_offset,
    )
    return result[0, :50], result[1, :50]


def solution(mesh):
    in_specs = (
        P(None, None, ("dom", "sub")),
        P(),
        P(None, None, ("dom", "sub")),
        P(("dom", "sub"), None),
        P(("dom", "sub"), None),
        P(("dom", "sub")),
        P(None, None, ("dom", "sub")),
        P(None, None, None, ("dom", "sub")),
        P(),
        P(None, ("dom", "sub")),
    )
    out_specs = (P(None, ("dom", "sub")), P(None, ("dom", "sub")))
    return jax.shard_map(
        per_device, mesh=mesh, in_specs=in_specs, out_specs=out_specs, check_vma=False
    )
```

```python
import functools

import jax
import jax.numpy as jnp
from jax import lax
from jax.experimental import pallas as pl
from jax.experimental.pallas import tpu as pltpu
from jax.sharding import PartitionSpec as P

MESH = pl.DeviceIdType.MESH
F32 = jnp.float32
BF16 = jnp.bfloat16

NZ = 16
NP = 32
NY = 4
ROWS = 50
PARTS = (2, 1, 3, 0)
HOPS = (
    ((2, 8), (1, 7), (-1, -7)),
    ((2, 5), (1, 4), (-2, -5), (-1, -4), (3, 6), (-3, -6)),
    ((2, 2), (1, 1), (-2, -2), (-1, -1), (3, 3), (-3, -3)),
)


def halves(value):
    high = value.astype(BF16)
    return high, (value - high.astype(F32)).astype(BF16)


def dot_nt(left, right):
    return lax.dot_general(left, right, (((1,), (1,)), ((), ())), preferred_element_type=F32)


def dot_nn(left, right):
    return lax.dot_general(left, right, (((1,), (0,)), ((), ())), preferred_element_type=F32)


def ones_where(mask):
    return jnp.where(mask, F32(1.0), F32(0.0))


def iota(shape, dim):
    return lax.broadcasted_iota(jnp.int32, shape, dim)


def kernel(
    residual_hbm,
    fine_basis_hbm,
    basis_hbm,
    donors_hbm,
    counts_hbm,
    positions_hbm,
    inverse_hbm,
    jacobian_hbm,
    lift_hbm,
    offsets_hbm,
    result,
    residual,
    fine_basis,
    basis,
    donors,
    counts,
    positions,
    inverse,
    jacobian,
    lift,
    offsets,
    masked,
    pair,
    spread,
    outbox,
    inbox,
    chunks,
    hop_in,
    group,
    group_pos,
    seats_to_pos,
    chooser,
    lift_rows,
    ends_high,
    ends_low,
    halo_low,
    halo_high,
    coupling,
    load_sem,
    plane_send,
    plane_recv,
    hop_send,
    hop_recv,
    group_send,
    group_recv,
    pos_send,
    pos_recv,
    halo_send,
    halo_recv,
):
    dom = lax.axis_index("dom")
    y = lax.axis_index("sub")
    x = lax.div(dom, 32)
    z = lax.rem(lax.div(dom, 2), NZ)
    core = lax.rem(dom, 2)
    block = dom * NY + y

    def plane_peer(step):
        far_x = lax.rem(x + lax.div(step, 8), 4)
        far_core = lax.rem(core + lax.div(step, 4), 2)
        far_y = lax.rem(y + step, NY)
        return ((far_x * NZ + z) * 2 + far_core, far_y)

    def ring_peer(step):
        return ((x * NZ + lax.rem(z + step, NZ)) * 2 + core, y)

    def group_peer(step):
        return (dom, lax.rem(y + step, NY))

    def line_peer(step):
        other = lax.rem(block + step, 512)
        return (lax.div(other, NY), lax.rem(other, NY))

    loads = [
        pltpu.make_async_copy(source, target, load_sem.at[n])
        for n, (source, target) in enumerate(
            (
                (donors_hbm, donors),
                (counts_hbm, counts),
                (fine_basis_hbm, fine_basis),
                (residual_hbm, residual),
                (basis_hbm, basis),
                (positions_hbm, positions),
                (offsets_hbm, offsets),
                (lift_hbm, lift),
                (jacobian_hbm, jacobian),
                (inverse_hbm, inverse),
            )
        )
    ]
    for load in loads:
        load.start()

    barrier = pltpu.get_barrier_semaphore()

    for step in (3, 13, 2, 14, 1, 15):
        pl.semaphore_signal(barrier, inc=1, device_id=ring_peer(step), device_id_type=MESH)

    def plane_steps(part, body):
        def turned(i, carry):
            body(part * 8 + lax.rem(i, 2) * 4 + lax.rem(2 + 3 * lax.div(i, 2), NY))
            return carry

        def near(step, carry):
            body(step)
            return carry

        if part:
            lax.fori_loop(0, 8, turned, 0)
        else:
            lax.fori_loop(1, 8, near, 0)

    def greet(step):
        pl.semaphore_signal(barrier, inc=1, device_id=plane_peer(step), device_id_type=MESH)

    for part in PARTS:
        plane_steps(part, greet)
    for step in (1, 511):
        pl.semaphore_signal(barrier, inc=1, device_id=line_peer(step), device_id_type=MESH)

    loads[0].wait()
    donor_row = jnp.concatenate([donors[k : k + 1, :] for k in range(4)], axis=1)
    owner = lax.shift_right_logical(donor_row, 7)
    seat = jnp.bitwise_and(donor_row, 127).astype(F32)
    owner_f = owner.astype(F32)
    columns = []
    for tile in range(8):
        row = owner_f[:, tile * 128 : (tile + 1) * 128]
        columns.append(jnp.broadcast_to(row, (128, 128)).T)
    earlier = iota((128, 128), 0) < iota((128, 128), 1)
    ranks = []
    for tile in range(8):
        row = owner_f[:, tile * 128 : (tile + 1) * 128]
        total = ones_where((columns[tile] == row) & earlier)
        for before in range(tile):
            total = total + ones_where(columns[before] == row)
        ranks.append(jnp.sum(total, axis=0, keepdims=True))
    rank = jnp.concatenate(ranks, axis=1).astype(jnp.int32)
    far_z = jnp.bitwise_and(lax.shift_right_logical(owner, 3), 15)
    step_x = jnp.bitwise_and(lax.shift_right_logical(owner, 7) - x + 4, 3)
    step_core = jnp.bitwise_and(lax.shift_right_logical(owner, 2) - core + 2, 1)
    step_y = jnp.bitwise_and(owner - y + 4, 3)
    plane_step = step_x * 8 + step_core * 4 + step_y
    order = jnp.bitwise_and(far_z - z + 11 + NZ, NZ - 1)
    slot = plane_step * 32 + lax.shift_right_logical(order, 1) * 4 + rank
    odd = jnp.bitwise_and(order, 1)
    slot_even = jnp.where(odd == 0, slot, -1)
    slot_odd = jnp.where(odd == 1, slot, -1)

    for load in loads[1:4]:
        load.wait()
    upper0 = counts[0:1, :]
    upper1 = upper0 + counts[1:2, :]
    upper2 = upper1 + counts[2:3, :]
    point = iota((64, 256), 0)
    inside = (
        point < upper0,
        (point >= upper0) & (point < upper1),
        (point >= upper1) & (point < upper2),
        point >= upper2,
    )
    spans = ((0, 32), (0, 64), (0, 64), (32, 64))
    fine = fine_basis[...].T
    for v in range(5):
        values = lax.dot_general(
            fine,
            residual[v],
            (((1,), (0,)), ((), ())),
            precision=lax.Precision.HIGHEST,
            preferred_element_type=F32,
        )
        for k in range(4):
            masked[k, v] = jnp.where(inside[k], values, F32(0.0))
    loads[4].wait()
    for a in range(10):
        for k in range(4):
            low, high = spans[k]
            product = basis[a, low:high, :][None] * masked[k, :, low:high, :]
            pair[a * 5 : a * 5 + 5, k * 256 : (k + 1) * 256] = jnp.sum(product, axis=1)
    pair[50:51, :] = seat
    pair[51:64, :] = jnp.zeros((13, 1024), F32)
    pair_high, pair_low = halves(pair[...])
    nothing = jnp.zeros((64, 1024), BF16)
    spread[0] = jnp.concatenate([pair_high, nothing, pair_low, nothing], axis=0)
    spread[1] = jnp.concatenate([nothing, pair_high, nothing, pair_low], axis=0)

    for part in PARTS:
        slots = iota((256, 1024), 0) + part * 256
        rows = dot_nt(ones_where(slots == slot_even).astype(BF16), spread[0])
        rows = rows + dot_nt(ones_where(slots == slot_odd).astype(BF16), spread[1])
        rows = rows[:, :128] + rows[:, 128:]
        outbox[part * 8 : (part + 1) * 8] = rows.reshape(8, 4, 8, 128)

    pl.semaphore_wait(barrier, 39)
    loads[5].wait()


    def pos_copy(step):
        return pltpu.make_async_remote_copy(
            src_ref=group_pos.at[0],
            dst_ref=group_pos.at[step],
            send_sem=pos_send.at[step],
            recv_sem=pos_recv.at[step],
            device_id=group_peer(step),
            device_id_type=MESH,
        )

    def plane_copy(half, step):
        return pltpu.make_async_remote_copy(
            src_ref=outbox.at[step, pl.ds(half * 2, 2)],
            dst_ref=inbox.at[pl.ds(half * 2, 2), step],
            send_sem=plane_send.at[half],
            recv_sem=plane_recv.at[half],
            device_id=plane_peer(step),
            device_id_type=MESH,
        )

    for half in range(2):
        for part in PARTS:
            plane_steps(part, lambda step, half=half: plane_copy(half, step).start())
    group_pos[0] = jnp.broadcast_to(positions[...], (8, 128))
    for step in range(1, NY):
        pos_copy(step).start()
    inbox[:, 0] = outbox[0]

    for load in loads[6:8]:
        load.wait()
    own = iota((1, 128), 1)
    for f in range(4):
        offset = offsets[f : f + 1, :]
        there = block * 128 + own + offset
        good = (offset != 0) & (there >= 0) & (there < 65536)
        near = own + offset
        beyond = jnp.where(near < 0, near + 256, near)
        wanted = jnp.where(good, beyond, -1)
        for half in range(2):
            source = iota((128, 128), 0) + half * 128
            chooser[half * 128 : half * 128 + 128, f * 128 : f * 128 + 128] = ones_where(
                source == wanted
            ).astype(BF16)
    row_v = lax.shift_right_logical(iota((80, 64), 0), 4)
    col = iota((80, 64), 1)
    fifth = jnp.zeros((80, 64), jnp.int32)
    for b in range(1, 10):
        fifth = fifth + jnp.where(col >= b * 5, 1, 0)
    same = (col - fifth * 5 == row_v) & (col < 50)
    take_a = ones_where(
        jnp.bitwise_and(iota((80, 10), 0), 15) == iota((80, 10), 1)
    ).astype(BF16)
    b_low = iota((10, 64), 0) * 5
    b_col = iota((10, 64), 1)
    take_b = ones_where((b_col >= b_low) & (b_col < b_low + 5)).astype(BF16)
    for f in range(4):
        for n, part in enumerate(halves(lift[:, f, :])):
            wide = dot_nn(dot_nn(take_a, part).astype(BF16), take_b)
            wide = jnp.where(same, wide, F32(0.0)).astype(BF16)
            lift_rows[f, n * 80 : n * 80 + 80, :] = jnp.concatenate([wide, wide], axis=1)
    def wait_plane(half, sems):
        whole = inbox.at[pl.ds(half * 2, 2), pl.ds(1, NP - 1)]
        pltpu.make_async_copy(whole, whole, sems.at[half]).wait()

    in_pair = jnp.bitwise_and(lax.shift_right_logical(iota((128, 256), 1), 2), 1)
    cell = iota((128, 256), 0).astype(F32)

    def gather(quarter):
        turned = inbox[quarter].reshape(256, 128).T
        high, low = halves(turned)
        for h in range(2):
            left = jnp.concatenate(
                [high[h * 64 : h * 64 + 64], low[h * 64 : h * 64 + 64]], axis=0
            )
            hit = cell == turned[h * 64 + 50 : h * 64 + 51, :]
            right = jnp.concatenate(
                [
                    ones_where(hit & (in_pair == 0)).astype(BF16),
                    ones_where(hit & (in_pair == 1)).astype(BF16),
                ],
                axis=0,
            )
            both = dot_nt(left, right)
            both = both[:64] + both[64:]
            for n in range(2):
                chunks[quarter * 4 + n * 2 + h] = both[:, n * 128 : n * 128 + 128]

    def chunk_of(relative):
        return (relative + 11) % 16

    def hop_copy(hop, n):
        step, relative = HOPS[hop][n]
        return pltpu.make_async_remote_copy(
            src_ref=chunks.at[chunk_of(relative), pl.ds(0, ROWS)],
            dst_ref=hop_in.at[hop, n],
            send_sem=hop_send.at[hop, n],
            recv_sem=hop_recv.at[hop, n],
            device_id=ring_peer(step % NZ),
            device_id_type=MESH,
        )

    def add_up(hop, members, relative):
        for n in members:
            hop_copy(hop, n).wait_recv()
            chunks[chunk_of(relative), 0:ROWS, :] += hop_in[hop, n]

    wait_plane(0, plane_recv)
    gather(0)
    for hop, n in ((0, 0), (0, 1), (1, 0)):
        hop_copy(hop, n).start()
    gather(1)
    for hop, n in ((0, 2), (1, 2), (1, 3)):
        hop_copy(hop, n).start()
    wait_plane(1, plane_recv)
    gather(3)
    hop_copy(1, 1).start()
    gather(2)
    for step in range(1, NY):
        pos_copy(step).wait_recv()
    place = iota((128, 128), 0) + block * 128
    for step in range(NY):
        seats_to_pos[:, step * 128 : step * 128 + 128] = ones_where(
            place == group_pos[step, 0:1, :]
        ).astype(BF16)

    add_up(0, (0, 1), 6)
    hop_copy(1, 4).start()
    add_up(0, (2,), -6)
    hop_copy(1, 5).start()
    for n in range(4):
        hop_copy(2, n).start()
    add_up(1, (0, 1, 4), 3)
    hop_copy(2, 4).start()
    add_up(1, (2, 3, 5), -3)
    hop_copy(2, 5).start()
    def group_copy(step):
        return pltpu.make_async_remote_copy(
            src_ref=group.at[0],
            dst_ref=group.at[step],
            send_sem=group_send.at[step],
            recv_sem=group_recv.at[step],
            device_id=group_peer(step),
            device_id_type=MESH,
        )

    add_up(2, (0, 1, 2, 3, 4, 5), 0)
    group[0] = chunks[chunk_of(0), 0:ROWS, :]
    for step in (2, 1, 3):
        group_copy(step).start()
    for load in loads[8:]:
        load.wait()
    for step in (1, 3, 2):
        group_copy(step).wait_recv()
    blank = jnp.zeros((14, 128), F32)
    wide = jnp.concatenate(
        [jnp.concatenate([group[step], blank], axis=0) for step in range(NY)], axis=1
    )
    high, low = halves(wide)
    coarse = dot_nt(jnp.concatenate([high, low], axis=0), seats_to_pos[...])
    coarse = (coarse[:64] + coarse[64:])[:50]
    result[0, 0:50, :] = coarse

    def apply_inverse(field):
        return jnp.sum(inverse[...] * field[None], axis=1)

    def halo_copy(it, up):
        return pltpu.make_async_remote_copy(
            src_ref=(ends_high if up else ends_low).at[it],
            dst_ref=(halo_low if up else halo_high).at[it],
            send_sem=halo_send.at[it, 0 if up else 1],
            recv_sem=halo_recv.at[it, 0 if up else 1],
            device_id=line_peer(1 if up else 511),
            device_id_type=MESH,
        )

    lane_part = lax.shift_right_logical(iota((16, 128), 1), 5)

    def packed(rows, from_part):
        total = jnp.zeros((16, 128), F32)
        for g in range(4):
            shift = (g - from_part) % 4 * 32
            group_rows = rows[g * 16 : g * 16 + 16]
            turned = pltpu.roll(group_rows, shift, 1) if shift else group_rows
            total = jnp.where(lane_part == g, turned, total)
        return total

    def unpacked(low_ends, high_ends):
        parts = []
        for g in range(4):
            low_shift = (3 - g) % 4 * 32
            high_shift = (4 - g) % 4 * 32
            low_rows = pltpu.roll(low_ends, low_shift, 1) if low_shift else low_ends
            high_rows = pltpu.roll(high_ends, high_shift, 1) if high_shift else high_ends
            parts.append(jnp.where(lane_part == 3, low_rows, jnp.where(lane_part == 0, high_rows, F32(0.0))))
        return jnp.concatenate(parts, axis=0)

    tail = jnp.zeros((14, 128), F32)
    coupling[0:50, :] = jnp.zeros((50, 128), F32)

    def sweep(it, carry):
        field = apply_inverse(result[0, 0:50, :] - coupling[0:50, :])
        result[1, 0:50, :] = field

        @pl.when(it < 2)
        def _():
            whole = jnp.concatenate([field, tail], axis=0)
            ends_high[it] = packed(whole, 3)
            ends_low[it] = packed(whole, 0)
            halo_copy(it, True).start()
            halo_copy(it, False).start()
            halo_copy(it, True).wait_recv()
            halo_copy(it, False).wait_recv()
            wide = jnp.concatenate([whole, unpacked(halo_low[it], halo_high[it])], axis=1)
            high, low = halves(wide)
            picked = dot_nn(jnp.concatenate([high, low], axis=0), chooser[...]).astype(BF16)
            lifted = []
            for f in range(4):
                both = dot_nn(lift_rows[f], picked[:, f * 128 : f * 128 + 128])
                lifted.append(both[:80] + both[80:])
            for w in range(5):
                total = jnp.zeros((16, 128), F32)
                for f in range(4):
                    for v in range(5):
                        total = total + lifted[f][v * 16 : v * 16 + 16] * jacobian[w, v, f : f + 1, :]
                coupling[pl.ds(w, 10, stride=5), :] = total[:10]

        return carry

    lax.fori_loop(0, 3, sweep, 0)

    for half in range(2):
        wait_plane(half, plane_send)
    for hop in range(3):
        for n in range(len(HOPS[hop])):
            hop_copy(hop, n).wait_send()
    for step in range(1, NY):
        pos_copy(step).wait_send()
        group_copy(step).wait_send()
    for it in range(2):
        halo_copy(it, True).wait_send()
        halo_copy(it, False).wait_send()


def per_device(
    fine_residual,
    fine_basis,
    coarse_basis,
    donor_cells,
    point_counts,
    solver_pos,
    block_inverse,
    face_jacobian,
    face_lift,
    face_offset,
):
    vmem = pl.BlockSpec(memory_space=pltpu.VMEM)
    hbm = pl.BlockSpec(memory_space=pl.ANY)
    dma = pltpu.SemaphoreType.DMA
    result = pl.pallas_call(
        kernel,
        out_shape=jax.ShapeDtypeStruct((2, 56, 128), F32),
        in_specs=[hbm] * 10,
        out_specs=vmem,
        scratch_shapes=[
            pltpu.VMEM((5, 35, 256), F32),
            pltpu.VMEM((35, 64), F32),
            pltpu.VMEM((10, 64, 256), F32),
            pltpu.VMEM((4, 256), jnp.int32),
            pltpu.VMEM((4, 256), jnp.int32),
            pltpu.VMEM((1, 128), jnp.int32),
            pltpu.VMEM((50, 50, 128), F32),
            pltpu.VMEM((5, 5, 4, 128), F32),
            pltpu.VMEM((10, 4, 10), F32),
            pltpu.VMEM((4, 128), jnp.int32),
            pltpu.VMEM((4, 5, 64, 256), F32),
            pltpu.VMEM((64, 1024), F32),
            pltpu.VMEM((2, 256, 1024), BF16),
            pltpu.VMEM((NP, 4, 8, 128), F32),
            pltpu.VMEM((4, NP, 8, 128), F32),
            pltpu.VMEM((NZ, 64, 128), F32),
            pltpu.VMEM((3, 6, ROWS, 128), F32),
            pltpu.VMEM((NY, ROWS, 128), F32),
            pltpu.VMEM((NY, 8, 128), jnp.int32),
            pltpu.VMEM((128, 512), BF16),
            pltpu.VMEM((256, 512), BF16),
            pltpu.VMEM((4, 160, 128), BF16),
            pltpu.VMEM((2, 16, 128), F32),
            pltpu.VMEM((2, 16, 128), F32),
            pltpu.VMEM((2, 16, 128), F32),
            pltpu.VMEM((2, 16, 128), F32),
            pltpu.VMEM((64, 128), F32),
            dma((10,)),
            dma((2,)),
            dma((2,)),
            dma((3, 6)),
            dma((3, 6)),
            dma((NY,)),
            dma((NY,)),
            dma((NY,)),
            dma((NY,)),
            dma((2, 2)),
            dma((2, 2)),
        ],
        compiler_params=pltpu.CompilerParams(
            collective_id=0, has_side_effects=True
        ),
    )(
        fine_residual.transpose(1, 0, 2),
        fine_basis.T,
        coarse_basis.transpose(1, 0, 2),
        donor_cells.T,
        point_counts.T,
        solver_pos.reshape(1, 128),
        block_inverse,
        face_jacobian.transpose(1, 2, 0, 3),
        face_lift.transpose(1, 0, 2),
        face_offset,
    )
    return result[0, :50], result[1, :50]


def solution(mesh):
    in_specs = (
        P(None, None, ("dom", "sub")),
        P(),
        P(None, None, ("dom", "sub")),
        P(("dom", "sub"), None),
        P(("dom", "sub"), None),
        P(("dom", "sub")),
        P(None, None, ("dom", "sub")),
        P(None, None, None, ("dom", "sub")),
        P(),
        P(None, ("dom", "sub")),
    )
    out_specs = (P(None, ("dom", "sub")), P(None, ("dom", "sub")))
    return jax.shard_map(
        per_device, mesh=mesh, in_specs=in_specs, out_specs=out_specs, check_vma=False
    )
```
